128 devices in a mesh: grp: 4 (over z), ocn: 32 (over y, x, core).
Axes of the slice: x: 4, y: 4, z: 4, core: 2. Of those that a mesh axis runs over, the one named last changes fastest.
Arguments:
- ocean_state: float32 [4, 80, 131072], P(None, None, ('grp', 'ocn')), may hold values from -6 to 6
- adv_coef: float32 [6, 131072], P(None, ('grp', 'ocn')), may hold values from 0 to 0.15
- neighbours: int32 [6, 131072], P(None, ('grp', 'ocn')), may hold values from -512 to 512, as said below
- active_levels: int32 [131072], P(('grp', 'ocn')), may hold values from 1 to 80
- boundary_level: int32 [131072], P(('grp', 'ocn')), may hold values from 1 to 80
- kpp_diff: float32 [80, 131072], P(None, ('grp', 'ocn')), may hold values from 0.3 to 30
- kpp_visc: float32 [80, 131072], P(None, ('grp', 'ocn')), may hold values from 0.3 to 30
- atm_flux: float32 [4, 262144], P(None, ('grp', 'ocn')), may hold values from -6 to 6
- pair_source: int32 [2097152], P(('grp', 'ocn')), may hold values from 0 to 2047
- pair_weight: float32 [2097152], P(('grp', 'ocn')), may hold values from 0.1 to 1
- pair_device: int32 [2097152, 1], P(('grp', 'ocn')), may hold values from 0 to 127; in each aligned block of 16384 rows (0 to 16383, 16384 to 32767, ...) at most 256 rows name the same one
- pair_cell: int32 [2097152], P(('grp', 'ocn')), may hold values from 0 to 1023
Outputs:
- ocean_after: float32 [4, 80, 131072], P(None, None, ('grp', 'ocn'))
- surface_flux: float32 [4, 131072], P(None, ('grp', 'ocn'))
The draws below stay inside these ranges and needn't reach their ends.
Inputs may be any that keep to these rules, and one draw needn't show every extreme that they name: neighbours[k, c] is never 0. `pair_device`: among the pairs of one device, at most 256 name the same device, and some device is named exactly 256 times.
All inputs are finite; a program needn't handle non-finite values.
Results may differ from the reference program's by a relative error of at most 0.0003.
Values sent between devices are 32-bit elements; how exact they have to be, the bound alone decides.
A program may use at most 128 MiB of HBM per device.

```python
import math
import jax
import jax.numpy as jnp
import numpy as np
from jax import lax

NFIELD = 4
NLEV = 80
NEI = 6
HW = 512
ADV_STEPS = 2
CELLS_DEV = 1024
AC_DEV = 2048
PAIRS_DEV = 16384
CAP = 256
NCELL = 131072
ATM = 262144
PAIRS = 2097152
DEVICES = 128


def draw_neighbours(key, part):
    total_cells = CELLS_DEV * DEVICES
    key_reach, key_flip = jax.random.split(key)
    reach = jax.random.randint(key_reach, (NEI, total_cells), 1, HW + 1)
    flip = jax.random.randint(key_flip, (NEI, total_cells), 0, 2) * 2 - 1
    offsets = reach * flip
    offsets = offsets.at[0, 0].set(HW).at[1, 0].set(-HW)
    return offsets.astype(jnp.int32)


def place_ends(values, stream_key, low, top_value):
    longest = values.shape.index(max(values.shape))
    spots = []
    for shift in (0, 1):
        where = [jax.random.randint(jax.random.fold_in(stream_key, axis), (), 0, length) for axis, length in enumerate(values.shape)]
        where[longest] = (where[longest] + shift) % values.shape[longest]
        spots.append(tuple(where))
    return values.at[spots[0]].set(low).at[spots[1]].set(top_value)


def block_scale(own_key, shape, shards, low, high):
    factor_of, own = 1.0, jax.random.fold_in(own_key, 6)
    for position, shards_of in shards:
        draws = jnp.exp(jax.random.uniform(jax.random.fold_in(own, position), (shards_of,), jnp.float32, low / len(shards), high / len(shards)))
        factor_of = factor_of * jnp.repeat(draws, shape[position] // shards_of).reshape([-1 if axis == position else 1 for axis in range(len(shape))])
    return factor_of


def routed_block(key, own, number, rows, amount, top, most, skew):
    ranking = jax.random.permutation(key, amount)
    heavy_load, common = load_shares(amount, rows * top, most, skew, True), load_shares(amount, rows * top, most, skew, False)
    places = jnp.arange(amount)

    def named(tallies, rotation):
        used = int((tallies > 0).sum())
        fixed = max(1, used // 4)
        moved = fixed + (places - fixed + rotation * (used - fixed)) % max(1, amount - fixed)
        return jnp.zeros((amount,), jnp.int32).at[ranking[jnp.where(places < fixed, places, moved)]].set(jnp.asarray(tallies, jnp.int32))

    tallies = jnp.where(number % 4 == 0, named(heavy_load, number // 4), named(common, number - number // 4 - 1))
    mixed = jax.random.permutation(jax.random.fold_in(own, 3), amount)
    donor, taker = mixed[0:amount // 2 * 2:2], mixed[1:amount // 2 * 2:2]
    slack = jnp.minimum(tallies[donor] - 1, most - tallies[taker]) // 2
    slack = jnp.where((donor == ranking[0]) | (taker == ranking[0]) | (tallies[taker] == 0), 0, jnp.maximum(slack, 0))
    moved = jax.random.randint(jax.random.fold_in(own, 4), (amount // 2,), 0, 1 << 20) % (slack + 1)
    tallies = tallies.at[donor].add(-moved).at[taker].add(moved)
    members = jnp.searchsorted(jnp.cumsum(tallies), jnp.arange(rows * top), side="right").astype(jnp.int32)
    table = members.reshape(top, rows).T
    table = table[jax.random.permutation(jax.random.fold_in(own, 1), rows)]
    rotation = jax.random.randint(jax.random.fold_in(own, 2), (rows, 1), 0, top)
    return jnp.take_along_axis(table, (jnp.arange(top)[None, :] + rotation) % top, axis=1)


def load_shares(count, total, most, lean, full):
    portions = [(1 << 20) // math.isqrt(grade ** lean) + 1 for grade in range(1, count + 1)]
    largest = most if full else min(most, max(-(-total // count), total * portions[0] // sum(portions)))
    least = 1 if total - largest >= count - 1 else 0
    given, surplus = [largest] + [least] * (count - 1), total - largest - least * (count - 1)
    while surplus > 0:
        candidates = [i for i in range(1, count) if given[i] < largest] or [i for i in range(1, count) if given[i] < most]
        whole, budget = sum([portions[i] for i in candidates]), surplus
        for i in candidates:
            extra = min(most - given[i], max(1, budget * portions[i] // whole), surplus)
            given[i] = given[i] + extra
            surplus = surplus - extra
    return np.array(given)


def gaussian(key, dims, scale, limit, shards=(), held_as=jnp.bfloat16):
    level = block_scale(key, dims, shards, -0.22, 0.18) if shards else 1.0
    array = jax.random.normal(key, dims, jnp.float32) * scale * level
    return jnp.minimum(jnp.maximum(array, -limit), limit).astype(held_as)


def setup_inputs(seed: int = 0) -> dict:
    seeds = jax.random.split(jax.random.key(seed), 13)
    ocean_state = gaussian(seeds[0], (NFIELD, NLEV, NCELL), 1.0, 6.0, ((2, 128),), jnp.float32)
    adv_coef = jnp.clip(0.15 * jax.random.uniform(seeds[1], (NEI, NCELL), jnp.float32) ** block_scale(seeds[1], (NEI, NCELL), ((1, 128),), -0.2, 0.2), 0.0, 0.15)
    neighbours = draw_neighbours(jax.random.fold_in(seeds[12], 71), 0)
    active_levels = place_ends(jax.random.randint(seeds[3], (NCELL,), 1, NLEV + 1), jax.random.fold_in(seeds[3], 1), 1, NLEV).astype(jnp.int32)
    boundary_level = place_ends(jax.random.randint(seeds[4], (NCELL,), 1, NLEV + 1), jax.random.fold_in(seeds[4], 1), 1, NLEV).astype(jnp.int32)
    kpp_diff = jnp.clip(jnp.exp(math.log(30.0) - 4.6051701 * jax.random.uniform(seeds[5], (NLEV, NCELL), jnp.float32) ** block_scale(seeds[5], (NLEV, NCELL), ((1, 128),), -0.2, 0.2)), 0.3, 30.0)
    kpp_visc = jnp.clip(jnp.exp(math.log(30.0) - 4.6051701 * jax.random.uniform(seeds[6], (NLEV, NCELL), jnp.float32) ** block_scale(seeds[6], (NLEV, NCELL), ((1, 128),), -0.2, 0.2)), 0.3, 30.0)
    atm_flux = gaussian(seeds[7], (NFIELD, ATM), 1.0, 6.0, ((1, 128),), jnp.float32)
    pair_source = place_ends(jax.random.randint(seeds[8], (PAIRS,), 0, AC_DEV), jax.random.fold_in(seeds[8], 1), 0, AC_DEV - 1).astype(jnp.int32)
    pair_weight = jnp.clip(0.1 + 0.9 * jax.random.uniform(seeds[9], (PAIRS,), jnp.float32) ** block_scale(seeds[9], (PAIRS,), ((0, 128),), -0.2, 0.2), 0.1, 1.0)
    pair_device_keys = jax.random.split(jax.random.fold_in(seeds[10], 1), PAIRS // PAIRS_DEV)
    pair_device_turns = jax.random.permutation(jax.random.fold_in(seeds[10], 3), PAIRS // PAIRS_DEV)
    pair_device = jax.vmap(lambda own, number: routed_block(jax.random.fold_in(seeds[10], 2), own, number, PAIRS_DEV, DEVICES, 1, CAP, 2))(pair_device_keys, pair_device_turns).reshape((PAIRS, 1))
    pair_cell = place_ends(jax.random.randint(seeds[11], (PAIRS,), 0, CELLS_DEV), jax.random.fold_in(seeds[11], 1), 0, CELLS_DEV - 1).astype(jnp.int32)
    return dict(ocean_state=ocean_state, adv_coef=adv_coef, neighbours=neighbours, active_levels=active_levels, boundary_level=boundary_level, kpp_diff=kpp_diff, kpp_visc=kpp_visc, atm_flux=atm_flux, pair_source=pair_source, pair_weight=pair_weight, pair_device=pair_device, pair_cell=pair_cell)


def advect(extended, edge_weights, gather_at, active, start, window):
    centre = extended[:, :, start:start + window]
    summed = centre
    for k in range(gather_at.shape[0]):
        summed = summed + edge_weights[k] * (jnp.take(extended, gather_at[k], axis=2) - centre)
    levels = jnp.arange(extended.shape[1], dtype=jnp.int32)[:, None]
    return jnp.where(levels < active[None, :], summed, centre)


def face_kappa(mixing_rate, boundary, active):
    levels = jnp.arange(mixing_rate.shape[0], dtype=jnp.int32)[:, None]
    inside = levels < boundary[None, :]
    open_face = (levels >= 1) & (levels < active[None, :])
    return jnp.where(open_face, jnp.where(inside, mixing_rate, 0.05), 0.0)


def mixing(prognostic, above_face, surface):
    below_face = jnp.concatenate([above_face[:, 1:], jnp.zeros_like(above_face[:, :1])], axis=1)
    right_side = prognostic.at[:, 0].add(surface)
    diagonal = 1.0 + above_face + below_face

    def forward(carried, inputs):
        ratio_prev, solved_prev = carried
        above_row, below_row, centre_row, right_row = inputs
        pivot_value = centre_row + above_row * ratio_prev
        ratio_next = -below_row / pivot_value
        solved_next = (right_row + above_row * solved_prev) / pivot_value
        return (ratio_next, solved_next), (ratio_next, solved_next)

    start_pair = (jnp.zeros_like(surface), jnp.zeros_like(surface))
    moved = tuple(jnp.moveaxis(a, 1, 0) for a in (above_face, below_face, diagonal, right_side))
    _, (ratios, eliminated) = lax.scan(forward, start_pair, moved)

    def backward(carried, inputs):
        ratio_row, solved_row = inputs
        result = solved_row - ratio_row * carried
        return result, result

    _, columns = lax.scan(backward, jnp.zeros_like(surface), (ratios, eliminated), reverse=True)
    return jnp.moveaxis(columns, 0, 1)


def reference(ocean_state, adv_coef, neighbours, active_levels, boundary_level, kpp_diff, kpp_visc, atm_flux, pair_source, pair_weight, pair_device, pair_cell):
    sender = jnp.arange(PAIRS, dtype=jnp.int32) // PAIRS_DEV
    column = sender * AC_DEV + pair_source
    contrib = atm_flux[:, column] * pair_weight[None, :]
    target = pair_device[:, 0] * CELLS_DEV + pair_cell
    surface_flux = jnp.zeros((NFIELD, NCELL), jnp.float32).at[:, target].add(contrib)
    diff_face = face_kappa(kpp_diff, boundary_level, active_levels)
    visc_face = face_kappa(kpp_visc, boundary_level, active_levels)
    cells = jnp.arange(NCELL, dtype=jnp.int32)[None, :]
    gather_at = jnp.mod(cells + neighbours, NCELL).astype(jnp.int32)
    results = []
    for f in range(NFIELD):
        prognostic = ocean_state[f][None]
        for s in range(ADV_STEPS):
            prognostic = advect(prognostic, adv_coef, gather_at, active_levels, 0, NCELL)
        chosen = diff_face if f < 2 else visc_face
        results.append(mixing(prognostic, chosen[None], surface_flux[f][None])[0])
    return jnp.stack(results), surface_flux
```

```python
import functools

import jax
import jax.numpy as jnp
from jax import lax
from jax.experimental import pallas as pl
from jax.experimental.pallas import tpu as pltpu
from jax.sharding import PartitionSpec as P

NFIELD = 4
NEI = 6
HW = 512
ADV_STEPS = 2
SLOTS = 256
LANES = 128
SLAB = 16
USED = 10
MESH = pl.DeviceIdType.MESH
F32 = jnp.float32
BF16 = jnp.bfloat16
I32 = jnp.int32


def iota(shape, dim):
    return lax.broadcasted_iota(I32, shape, dim)


def nt_dot(a, b):
    return lax.dot_general(a, b, (((1,), (1,)), ((), ())), preferred_element_type=F32)


def pack_kernel(n, dev_ref, src_ref, cell_ref, w_ref, atm_ref, out_ref, acc, carry, tabs):
    chunk = 8
    acc[...] = jnp.zeros_like(acc)
    carry[...] = jnp.zeros_like(carry)
    ntab = atm_ref.shape[1] // LANES
    for f in range(NFIELD):
        for r in range(ntab):
            tabs[f * ntab + r] = jnp.broadcast_to(
                atm_ref[f : f + 1, r * LANES : (r + 1) * LANES], (8, LANES)
            )
    iota_d = iota((n, LANES), 0)
    iota_r = iota((SLOTS, LANES), 0).astype(F32)
    tri = jnp.where(iota((256, 256), 0) <= iota((256, 256), 1), 1.0, 0.0).astype(BF16)

    def one_chunk(i, _):
        at = pl.ds(pl.multiple_of(i * chunk, chunk), chunk)
        dest = dev_ref[at, :]
        code = src_ref[at, :] * 1024 + cell_ref[at, :]
        weight = w_ref[at, :]
        high = weight.astype(BF16).astype(F32)
        pieces = [
            (code & 127).astype(F32),
            ((code >> 7) & 127).astype(F32),
            (code >> 14).astype(F32),
            high,
            weight - high,
        ]
        run = carry[...]
        left = [[] for _ in pieces]
        right = []
        for s in range(0, chunk, 2):
            hit = [iota_d == dest[s + h : s + h + 1, :] for h in range(2)]
            member = jnp.concatenate(
                [jnp.where(m, 1.0, 0.0) for m in hit], axis=1
            ).astype(BF16)
            count = jnp.dot(member, tri, preferred_element_type=F32)
            for h in range(2):
                upto = count[:, h * LANES : (h + 1) * LANES] + run
                rank = jnp.sum(jnp.where(hit[h], upto, 0.0), axis=0, keepdims=True) - 1.0
                right.append(jnp.where(iota_r == rank, 1.0, 0.0).astype(BF16))
            run = run + jnp.broadcast_to(count[:, 255:256], (n, LANES))
            spread = member.reshape(n // 16, 16, 2 * LANES)
            for v, piece in enumerate(pieces):
                row = jnp.concatenate(
                    [
                        jnp.broadcast_to(piece[s + h : s + h + 1, :], (16, LANES))
                        for h in range(2)
                    ],
                    axis=1,
                ).astype(BF16)
                left[v].append((spread * row[None]).reshape(n, 2 * LANES))
        carry[...] = run
        lhs = jnp.concatenate([jnp.concatenate(part, axis=1) for part in left], axis=0)
        acc[...] += nt_dot(lhs, jnp.concatenate(right, axis=1))
        return 0

    lax.fori_loop(0, dev_ref.shape[0] // chunk, one_chunk, 0)

    def one_tile(t, _):
        for h in range(2):
            lanes = slice(h * LANES, (h + 1) * LANES)

            def part(v):
                return acc[pl.ds(pl.multiple_of(v * n + t * 8, 8), 8), lanes]

            code = (part(0) + part(1) * 128.0 + part(2) * 16384.0).astype(I32)
            weight = part(3) + part(4)
            cell = (code & 1023).astype(F32)
            source = code >> 10
            low = source & (LANES - 1)
            high = source >> 7
            values = [jnp.zeros((8, LANES), F32) for _ in range(NFIELD)]
            for r in range(ntab):
                here = high == r
                for f in range(NFIELD):
                    got = jnp.take_along_axis(tabs[f * ntab + r], low, axis=1)
                    values[f] = jnp.where(here, got, values[f])
            for f in range(NFIELD):
                out_ref[pl.ds(t * 8 * SLAB + f * 2 + h, 8, stride=SLAB), :] = values[f] * weight
            out_ref[pl.ds(t * 8 * SLAB + 8 + h, 8, stride=SLAB), :] = cell
        return 0

    lax.fori_loop(0, n // 8, one_tile, 0)


def move_kernel(
    n, n_inner, levels, cells,
    q_ref, coef_ref, nb_ref, act_ref, act8_ref, bl8_ref, kd_ref, kv_ref, packed_ref,
    z_ref, e_ref, r0_ref, recv_ref,
    halo, q1, split, sten_h, sten_l, rates, recip, rows,
    halo_send, halo_recv, slab_send, slab_recv, own_sem,
):
    rows_all = NFIELD * levels
    me = lax.axis_index("grp") * n_inner + lax.axis_index("ocn")

    def ident(d):
        return (d // n_inner, lax.rem(d, n_inner))

    right = lax.rem(me + 1, n)
    left = lax.rem(me + n - 1, n)
    barrier = pltpu.get_barrier_semaphore()

    def greet(i, _):
        pl.semaphore_signal(
            barrier, inc=1, device_id=ident(lax.rem(me + i, n)), device_id_type=MESH
        )
        return 0

    lax.fori_loop(1, n, greet, 0)
    pl.semaphore_wait(barrier, n - 1)

    def halo_copies(step, source):
        to_left = pltpu.make_async_remote_copy(
            src_ref=source.at[:, :, pl.ds(0, HW)],
            dst_ref=halo.at[step, 1],
            send_sem=halo_send.at[step, 0],
            recv_sem=halo_recv.at[step, 1],
            device_id=ident(left),
            device_id_type=MESH,
        )
        to_right = pltpu.make_async_remote_copy(
            src_ref=source.at[:, :, pl.ds(cells - HW, HW)],
            dst_ref=halo.at[step, 0],
            send_sem=halo_send.at[step, 1],
            recv_sem=halo_recv.at[step, 0],
            device_id=ident(right),
            device_id_type=MESH,
        )
        return to_left, to_right

    first = halo_copies(0, q_ref)
    first[0].start()
    first[1].start()

    def slab_copy(d):
        return pltpu.make_async_remote_copy(
            src_ref=packed_ref.at[pl.ds(pl.multiple_of(d * SLAB, 8), SLAB), :],
            dst_ref=recv_ref.at[pl.ds(pl.multiple_of(me * SLAB, 8), SLAB), :],
            send_sem=slab_send,
            recv_sem=slab_recv,
            device_id=ident(d),
            device_id_type=MESH,
        )

    def send_slab(i, _):
        slab_copy(lax.rem(me + i, n)).start()
        return 0

    lax.fori_loop(1, n, send_slab, 0)
    mine = pl.ds(pl.multiple_of(me * SLAB, 8), SLAB)
    own = pltpu.make_async_copy(packed_ref.at[mine, :], recv_ref.at[mine, :], own_sem)
    own.start()

    block = 256
    band = block + 2 * HW
    offset = [nb_ref[k : k + 1, :] for k in range(NEI)]
    weight = [coef_ref[k : k + 1, :] for k in range(NEI)]
    total = weight[0]
    for k in range(1, NEI):
        total = total + weight[k]
    merged = []
    for k in range(NEI):
        w = weight[k]
        for j in range(k):
            w = w + jnp.where(offset[j] == offset[k], weight[j], 0.0)
        merged.append(w)
    rows[0:1, :] = total
    local = lax.rem(iota((1, cells), 1), block) + HW
    target = [local + offset[k] for k in range(NEI)]
    for b in range(cells // block):
        cols = slice(b * block, (b + 1) * block)
        aim = [t[:, cols] for t in target]
        put = [w[:, cols] for w in merged]

        def one_band(i, _):
            at = pl.ds(pl.multiple_of(i * 128, 128), 128)
            row = iota((128, block), 0) + i * 128
            value = jnp.zeros((128, block), F32)
            for k in range(NEI):
                value = jnp.where(row == aim[k], put[k], value)
            high = value.astype(BF16)
            sten_h[b, at, :] = high
            sten_l[b, at, :] = (value - high.astype(F32)).astype(BF16)
            return 0

        lax.fori_loop(0, band // 128, one_band, 0)

    def put_split(field, lanes, value):
        high = value.astype(BF16)
        split[pl.ds(field * levels, levels), lanes] = high
        split[pl.ds(rows_all + field * levels, levels), lanes] = (
            value - high.astype(F32)
        ).astype(BF16)

    for f in range(NFIELD):
        put_split(f, pl.ds(HW, cells), q_ref[f])

    tiles = cells // LANES
    for j in range(tiles):
        lanes = slice(j * LANES, (j + 1) * LANES)
        rates[pl.ds(j, levels, stride=tiles), :] = kd_ref[:, lanes]
        rates[pl.ds(levels * tiles + j, levels, stride=tiles), :] = kv_ref[:, lanes]
    active8 = act8_ref[...]
    bound8 = bl8_ref[...]

    def one_level(i, below):
        level = levels - 1 - i
        is_open = (active8 > level) & (level >= 1)
        inside = bound8 > level
        after = []
        for c in range(2):
            at = pl.ds(pl.multiple_of((c * levels + level) * tiles, 8), tiles)
            face = jnp.where(is_open, jnp.where(inside, rates[at, :], 0.05), 0.0)
            inverse = 1.0 / (1.0 + face + below[c])
            ratio = face * inverse
            recip[at, :] = inverse
            e_ref[at, :] = ratio
            after.append(face - face * ratio)
        return tuple(after)

    nothing = jnp.zeros((tiles, LANES), F32)
    lax.fori_loop(0, levels, one_level, (nothing, nothing), unroll=4)
    for c in range(2):
        r0_ref[c * tiles : (c + 1) * tiles, :] = recip[pl.ds(c * levels * tiles, tiles), :]

    def transport(b, source):
        window = pl.ds(b * block, band)
        both = jnp.dot(split[:, window], sten_h[b], preferred_element_type=F32)
        extra = jnp.dot(split[:rows_all, window], sten_l[b], preferred_element_type=F32)
        inflow = both[:rows_all] + both[rows_all:] + extra
        cols = slice(b * block, (b + 1) * block)
        live = iota((levels, block), 0) < act_ref[:, cols]
        out = []
        for f in range(NFIELD):
            centre = source[f, :, cols]
            moved = centre + inflow[f * levels : (f + 1) * levels] - centre * rows[0:1, cols]
            out.append(jnp.where(live, moved, centre))
        return out

    nblock = cells // block
    for step in range(ADV_STEPS):
        copies = first if step == 0 else second
        for side in range(2):
            copies[1 - side].wait_recv()
            for f in range(NFIELD):
                put_split(f, pl.ds(0 if side == 0 else HW + cells, HW), halo[step, side, f])
            for b in range(side * nblock // 2, (side + 1) * nblock // 2):
                got = transport(b, q_ref if step == 0 else q1)
                for f in range(NFIELD):
                    if step == 0:
                        q1[f, :, b * block : (b + 1) * block] = got[f]
                    else:
                        for h in range(block // LANES):
                            z_ref[
                                pl.ds(f * levels * tiles + b * (block // LANES) + h, levels, stride=tiles), :
                            ] = got[f][:, h * LANES : (h + 1) * LANES]
            if step == 0:
                if side == 0:
                    second = halo_copies(1, q1)
                second[side].start()
        copies[0].wait_send()
        copies[1].wait_send()
        if step == 0:
            for f in range(NFIELD):
                put_split(f, pl.ds(HW, cells), q1[f])

    def lift(i, above):
        level = levels - 1 - i
        after = []
        for f in range(NFIELD):
            at = pl.ds(pl.multiple_of((f * levels + level) * tiles, 8), tiles)
            own_at = pl.ds(pl.multiple_of((f // 2 * levels + level) * tiles, 8), tiles)
            right_side = z_ref[at, :] + above[f]
            z_ref[at, :] = recip[own_at, :] * right_side
            after.append(e_ref[own_at, :] * right_side)
        return tuple(after)

    lax.fori_loop(0, levels, lift, (nothing,) * NFIELD, unroll=4)

    own.wait()
    everyone = pl.ds(0, (n - 1) * SLAB)
    arrived = pltpu.make_async_remote_copy(
        src_ref=packed_ref.at[everyone, :],
        dst_ref=recv_ref.at[everyone, :],
        send_sem=slab_send,
        recv_sem=slab_recv,
        device_id=ident(right),
        device_id_type=MESH,
    )
    arrived.wait_send()
    arrived.wait_recv()


def finish_kernel(n, levels, cells, z_ref, e_ref, r0_ref, recv_ref, out_ref, surface_ref, state, acc):
    tiles = cells // LANES
    group = 4
    acc[...] = jnp.zeros_like(acc)
    iota_a = iota((tiles, LANES), 0)
    iota_b = iota((LANES, LANES), 0)

    def some_slabs(i, _):
        left = [[] for _ in range(2 * NFIELD)]
        right = []
        for s in range(group):
            base = pl.multiple_of((i * group + s) * SLAB, 8)
            values = recv_ref[pl.ds(base, 8), :]
            cell = recv_ref[pl.ds(base + 8, 8), :].astype(I32)
            for h in range(2):
                at = cell[h : h + 1, :]
                hit = iota_a == (at >> 7)
                right.append(jnp.where(iota_b == (at & 127), 1.0, 0.0).astype(BF16))
                for f in range(NFIELD):
                    value = jnp.where(hit, values[f * 2 + h : f * 2 + h + 1, :], 0.0)
                    high = value.astype(BF16).astype(F32)
                    left[f].append(high)
                    left[NFIELD + f].append(value - high)
        lhs = jnp.concatenate([jnp.concatenate(part, axis=1) for part in left], axis=0)
        acc[...] += nt_dot(lhs.astype(BF16), jnp.concatenate(right, axis=1))
        return 0

    lax.fori_loop(0, n // group, some_slabs, 0)
    half = NFIELD * tiles
    below = []
    for f in range(NFIELD):
        at = pl.ds(f * tiles, tiles)
        surface = acc[at, :] + acc[pl.ds(half + f * tiles, tiles), :]
        for a in range(tiles):
            surface_ref[f : f + 1, a * LANES : (a + 1) * LANES] = surface[a : a + 1, :]
        c = f // 2
        top = z_ref[pl.ds(f * levels * tiles, tiles), :] + surface * r0_ref[c * tiles : (c + 1) * tiles, :]
        state[pl.ds(f * levels * tiles, tiles), :] = top
        below.append(top)

    def drop(level, above):
        after = []
        for f in range(NFIELD):
            at = pl.ds(pl.multiple_of((f * levels + level) * tiles, 8), tiles)
            own_at = pl.ds(pl.multiple_of((f // 2 * levels + level) * tiles, 8), tiles)
            value = z_ref[at, :] + e_ref[own_at, :] * above[f]
            state[at, :] = value
            after.append(value)
        return tuple(after)

    lax.fori_loop(1, levels, drop, tuple(below), unroll=4)
    for f in range(NFIELD):
        for j in range(tiles):
            out_ref[f, :, j * LANES : (j + 1) * LANES] = state[
                pl.ds(f * levels * tiles + j, levels, stride=tiles), :
            ]


def vmem(count):
    return [pl.BlockSpec(memory_space=pltpu.VMEM)] * count


def shaped(*shape):
    return jax.ShapeDtypeStruct(shape, F32)


def per_device(
    n, n_inner,
    ocean_state, adv_coef, neighbours, active_levels, boundary_level, kpp_diff, kpp_visc,
    atm_flux, pair_source, pair_weight, pair_device, pair_cell,
):
    levels, cells = ocean_state.shape[1:]
    tiles = cells // LANES
    pairs = pair_source.shape[0]
    wide = (pairs // LANES, LANES)
    limit = 56 * 1024 * 1024
    packed = pl.pallas_call(
        functools.partial(pack_kernel, n),
        out_shape=shaped(n * SLAB, LANES),
        in_specs=vmem(5),
        out_specs=vmem(1)[0],
        scratch_shapes=[
            pltpu.VMEM((5 * n, SLOTS), F32),
            pltpu.VMEM((n, LANES), F32),
            pltpu.VMEM((NFIELD * atm_flux.shape[1] // LANES, 8, LANES), F32),
        ],
        compiler_params=pltpu.CompilerParams(vmem_limit_bytes=limit),
        name="pack",
    )(
        pair_device.reshape(wide), pair_source.reshape(wide), pair_cell.reshape(wide),
        pair_weight.reshape(wide), atm_flux,
    )
    rows_all = NFIELD * levels
    band = 256 + 2 * HW
    z, e, r0, received = pl.pallas_call(
        functools.partial(move_kernel, n, n_inner, levels, cells),
        out_shape=(
            shaped(rows_all * tiles, LANES),
            shaped(2 * levels * tiles, LANES),
            shaped(2 * tiles, LANES),
            shaped(n * SLAB, LANES),
        ),
        in_specs=vmem(9),
        out_specs=tuple(vmem(4)),
        scratch_shapes=[
            pltpu.VMEM((ADV_STEPS, 2, NFIELD, levels, HW), F32),
            pltpu.VMEM((NFIELD, levels, cells), F32),
            pltpu.VMEM((2 * rows_all, cells + 2 * HW), BF16),
            pltpu.VMEM((cells // 256, band, 256), BF16),
            pltpu.VMEM((cells // 256, band, 256), BF16),
            pltpu.VMEM((2 * levels * tiles, LANES), F32),
            pltpu.VMEM((2 * levels * tiles, LANES), F32),
            pltpu.VMEM((8, cells), F32),
            pltpu.SemaphoreType.DMA((ADV_STEPS, 2)),
            pltpu.SemaphoreType.DMA((ADV_STEPS, 2)),
            pltpu.SemaphoreType.DMA,
            pltpu.SemaphoreType.DMA,
            pltpu.SemaphoreType.DMA,
        ],
        compiler_params=pltpu.CompilerParams(
            vmem_limit_bytes=limit, collective_id=0, has_side_effects=True
        ),
        name="move",
    )(
        ocean_state, adv_coef, neighbours, active_levels.reshape(1, cells),
        active_levels.reshape(tiles, LANES), boundary_level.reshape(tiles, LANES),
        kpp_diff, kpp_visc, packed,
    )
    return pl.pallas_call(
        functools.partial(finish_kernel, n, levels, cells),
        out_shape=(shaped(NFIELD, levels, cells), shaped(NFIELD, cells)),
        in_specs=vmem(4),
        out_specs=tuple(vmem(2)),
        scratch_shapes=[
            pltpu.VMEM((rows_all * tiles, LANES), F32),
            pltpu.VMEM((2 * NFIELD * tiles, LANES), F32),
        ],
        compiler_params=pltpu.CompilerParams(vmem_limit_bytes=limit),
        name="finish",
    )(z, e, r0, received)


def solution(mesh):
    both = ("grp", "ocn")
    placed = (
        P(None, None, both), P(None, both), P(None, both), P(both), P(both), P(None, both),
        P(None, both), P(None, both), P(both), P(both), P(both, None), P(both),
    )
    n_inner = mesh.shape["ocn"]
    return jax.shard_map(
        functools.partial(per_device, mesh.shape["grp"] * n_inner, n_inner),
        mesh=mesh,
        in_specs=placed,
        out_specs=(P(None, None, both), P(None, both)),
        check_vma=False,
    )
```

```python
import functools

import jax
import jax.numpy as jnp
from jax import lax
from jax.experimental import pallas as pl
from jax.experimental.pallas import tpu as pltpu
from jax.sharding import PartitionSpec as P

NFIELD = 4
NEI = 6
HW = 512
ADV_STEPS = 2
SLOTS = 256
LANES = 128
SLAB = 16
USED = 10
BLOCK = 256
BAND = BLOCK + 2 * HW
MESH = pl.DeviceIdType.MESH
F32 = jnp.float32
BF16 = jnp.bfloat16
I32 = jnp.int32


def iota(shape, dim):
    return lax.broadcasted_iota(I32, shape, dim)


def nt_dot(a, b):
    return lax.dot_general(a, b, (((1,), (1,)), ((), ())), preferred_element_type=F32)


def thick(row, count):
    sixteen = jnp.broadcast_to(row, (16, LANES)).astype(BF16)
    return jnp.broadcast_to(sixteen[None], (count // 16, 16, LANES)).reshape(count, LANES)


def rank_phase(n, dev_ref, ranks, chunk):
    iota_d = iota((n, LANES), 0)
    tri = jnp.where(iota((256, 256), 0) <= iota((256, 256), 1), 1.0, 0.0).astype(BF16)

    def some(i, run):
        at = pl.ds(pl.multiple_of(i * chunk, 8), chunk)
        dest = dev_ref[at, :]
        out = []
        for s in range(0, chunk, 2):
            hit = [iota_d == dest[s + h : s + h + 1, :] for h in range(2)]
            member = jnp.concatenate([jnp.where(m, 1.0, 0.0) for m in hit], axis=1).astype(BF16)
            count = jnp.dot(member, tri, preferred_element_type=F32)
            for h in range(2):
                upto = count[:, h * LANES : (h + 1) * LANES] + run
                out.append(jnp.sum(jnp.where(hit[h], upto, 0.0), axis=0, keepdims=True) - 1.0)
            run = run + jnp.broadcast_to(count[:, 255:256], (n, LANES))
        ranks[at, :] = jnp.concatenate(out, axis=0)
        return run

    lax.fori_loop(0, dev_ref.shape[0] // chunk, some, jnp.zeros((n, LANES), F32))


def place_phase(n, dev_ref, src_ref, cell_ref, w_ref, ranks, acc, chunk):
    one, zero = jnp.ones((), BF16), jnp.zeros((), BF16)
    iota_d = iota((n, LANES), 0).astype(F32).astype(BF16)
    iota_r = iota((SLOTS, LANES), 0).astype(F32).astype(BF16)
    acc[...] = jnp.zeros_like(acc)

    def some(i, _):
        at = pl.ds(pl.multiple_of(i * chunk, 8), chunk)
        dest = dev_ref[at, :].astype(F32)
        code = src_ref[at, :] * 1024 + cell_ref[at, :]
        weight = w_ref[at, :]
        rank = ranks[at, :]
        high = weight.astype(BF16).astype(F32)
        pieces = [
            (code & 127).astype(F32),
            ((code >> 7) & 127).astype(F32),
            (code >> 14).astype(F32),
            high,
            weight - high,
        ]
        left = [[] for _ in pieces]
        right = []
        for s in range(chunk):
            mask = iota_d == thick(dest[s : s + 1, :], n)
            right.append(jnp.where(iota_r == thick(rank[s : s + 1, :], SLOTS), one, zero))
            for v, piece in enumerate(pieces):
                left[v].append(jnp.where(mask, thick(piece[s : s + 1, :], n), zero))
        lhs = jnp.concatenate([jnp.concatenate(part, axis=1) for part in left], axis=0)
        acc[...] += nt_dot(lhs, jnp.concatenate(right, axis=1))
        return 0

    lax.fori_loop(0, dev_ref.shape[0] // chunk, some, 0)


def gather_phase(n, me, atm_ref, acc, out_ref, tabs, send):
    ntab = atm_ref.shape[1] // LANES
    tiles = 2
    trips = n // (8 * tiles)
    for f in range(NFIELD):
        for r in range(ntab):
            tabs[f * ntab + r] = jnp.broadcast_to(
                atm_ref[f : f + 1, r * LANES : (r + 1) * LANES], (8, LANES)
            )

    def some(i, _):
        turn = lax.rem(i + me // (8 * tiles), trips)
        todo = []
        for u in range(tiles):
            t = turn * tiles + u
            for h in range(2):
                lanes = slice(h * LANES, (h + 1) * LANES)

                def part(v):
                    return acc[pl.ds(pl.multiple_of(v * n + t * 8, 8), 8), lanes]

                code = (part(0) + part(1) * 128.0 + part(2) * 16384.0).astype(I32)
                weight = part(3) + part(4)
                source = code >> 10
                todo.append(
                    (t, h, weight, source & (LANES - 1), source >> 7,
                     [jnp.zeros((8, LANES), F32)] * NFIELD)
                )
                out_ref[pl.ds(t * 8 * SLAB + 8 + h, 8, stride=SLAB), :] = (code & 1023).astype(F32)
        for r in range(ntab):
            for t, h, weight, low, high, values in todo:
                here = high == r
                for f in range(NFIELD):
                    got = jnp.take_along_axis(tabs[f * ntab + r], low, axis=1)
                    values[f] = jnp.where(here, got, values[f])
        for t, h, weight, low, high, values in todo:
            for f in range(NFIELD):
                out_ref[pl.ds(t * 8 * SLAB + f * 2 + h, 8, stride=SLAB), :] = values[f] * weight

        def each(j, _):
            send(turn * 8 * tiles + lax.rem(j + me, 8 * tiles))
            return 0

        lax.fori_loop(0, 8 * tiles, each, 0)
        return 0

    lax.fori_loop(0, trips, some, 0)


def scatter_phase(n, recv_ref, acc, group):
    one, zero = jnp.ones((), BF16), jnp.zeros((), BF16)
    acc[...] = jnp.zeros_like(acc)
    iota_a = (iota((16, LANES), 0) & 7).astype(F32).astype(BF16)
    iota_b = iota((LANES, LANES), 0).astype(F32).astype(BF16)

    def some(i, _):
        left = [[] for _ in range(4)]
        right = []
        for s in range(group):
            base = pl.multiple_of((i * group + s) * SLAB, 8)
            values = recv_ref[pl.ds(base, 8), :]
            cell = recv_ref[pl.ds(base + 8, 8), :].astype(I32)
            high = values.astype(BF16).astype(F32)
            low = values - high
            major = (cell >> 7).astype(F32)
            minor = (cell & 127).astype(F32)
            for h in range(2):
                hit = iota_a == jnp.broadcast_to(major[h : h + 1, :], (16, LANES)).astype(BF16)
                right.append(jnp.where(iota_b == thick(minor[h : h + 1, :], LANES), one, zero))
                for p, piece in enumerate((high, low)):
                    for g in range(2):
                        pair = jnp.concatenate(
                            [
                                jnp.broadcast_to(piece[f * 2 + h : f * 2 + h + 1, :], (8, LANES))
                                for f in (2 * g, 2 * g + 1)
                            ],
                            axis=0,
                        ).astype(BF16)
                        left[p * 2 + g].append(jnp.where(hit, pair, zero))
        lhs = jnp.concatenate([jnp.concatenate(part, axis=1) for part in left], axis=0)
        acc[...] += nt_dot(lhs, jnp.concatenate(right, axis=1))
        return 0

    lax.fori_loop(0, n // group, some, 0)


def stencil_phase(cells, coef_ref, nb_ref, total_ref, sten_h, sten_l):
    offset = [nb_ref[k : k + 1, :] for k in range(NEI)]
    weight = [coef_ref[k : k + 1, :] for k in range(NEI)]
    total = weight[0]
    for k in range(1, NEI):
        total = total + weight[k]
    total_ref[0:1, :] = total
    merged = []
    for k in range(NEI):
        w = weight[k]
        for j in range(k):
            w = w + jnp.where(offset[j] == offset[k], weight[j], 0.0)
        merged.append(w)
    local = lax.rem(iota((1, cells), 1), BLOCK) + HW
    target = [local + offset[k] for k in range(NEI)]
    for b in range(cells // BLOCK):
        cols = slice(b * BLOCK, (b + 1) * BLOCK)
        aim = [t[:, cols] for t in target]
        put = [w[:, cols] for w in merged]

        def one_band(i, _):
            at = pl.ds(pl.multiple_of(i * 128, 128), 128)
            row = iota((128, BLOCK), 0) + i * 128
            value = jnp.zeros((128, BLOCK), F32)
            for k in range(NEI):
                value = jnp.where(row == aim[k], put[k], value)
            high = value.astype(BF16)
            sten_h[b, at, :] = high
            sten_l[b, at, :] = (value - high.astype(F32)).astype(BF16)
            return 0

        lax.fori_loop(0, BAND // 128, one_band, 0)


def move_kernel(
    n, n_inner, levels, cells,
    dev_ref, src_ref, cell_ref, w_ref, atm_ref,
    q_ref, coef_ref, nb_ref, act_ref, act8_ref, bl8_ref, kd_ref, kv_ref,
    z_ref, e_ref, r0_ref, surface_ref,
    ranks, slots, tabs, packed, received, surface_acc,
    halo, q1, split, sten_h, sten_l, rates, recip, total_ref,
    halo_send, halo_recv, slab_send, slab_recv, own_sem,
):
    tiles = cells // LANES
    me = lax.axis_index("grp") * n_inner + lax.axis_index("ocn")
    group_rows = NFIELD // 2 * levels

    def ident(d):
        return (d // n_inner, lax.rem(d, n_inner))

    barrier = pltpu.get_barrier_semaphore()

    def greet(i, _):
        pl.semaphore_signal(
            barrier, inc=1, device_id=ident(lax.rem(me + i, n)), device_id_type=MESH
        )
        return 0

    lax.fori_loop(1, n, greet, 0)
    rank_phase(n, dev_ref, ranks, 32)

    def put_split(f, lanes, value):
        g = f // 2
        at = g * 2 * group_rows + (f % 2) * levels
        high = value.astype(BF16)
        split[pl.ds(at, levels), lanes] = high
        split[pl.ds(at + group_rows, levels), lanes] = (value - high.astype(F32)).astype(BF16)

    for f in range(NFIELD):
        put_split(f, pl.ds(HW, cells), q_ref[f])
    pl.semaphore_wait(barrier, n - 1)

    far = lax.rem(me, 2)
    near = 1 - far

    def halo_copy(step, side, g):
        source = q_ref if step == 0 else q1
        fields = pl.ds(2 * g, 2)
        return pltpu.make_async_remote_copy(
            src_ref=source.at[fields, :, pl.ds(pl.multiple_of(side * HW, HW), HW)],
            dst_ref=halo.at[step, 1 - side, fields],
            send_sem=halo_send.at[step, side, g],
            recv_sem=halo_recv.at[step, 1 - side, g],
            device_id=ident(lax.rem(me + n - 1 + 2 * side, n)),
            device_id_type=MESH,
        )

    for side in (far, near):
        for g in range(2):
            halo_copy(0, side, g).start()
    place_phase(n, dev_ref, src_ref, cell_ref, w_ref, ranks, slots, 32)

    def slab_copy(d):
        return pltpu.make_async_remote_copy(
            src_ref=packed.at[pl.ds(pl.multiple_of(d * SLAB, 8), USED), :],
            dst_ref=received.at[pl.ds(pl.multiple_of(me * SLAB, 8), USED), :],
            send_sem=slab_send,
            recv_sem=slab_recv,
            device_id=ident(d),
            device_id_type=MESH,
        )

    def send_slab(d):
        @pl.when(d != me)
        def _():
            slab_copy(d).start()

    gather_phase(n, me, atm_ref, slots, packed, tabs, send_slab)
    mine = pl.ds(pl.multiple_of(me * SLAB, 8), SLAB)
    own = pltpu.make_async_copy(packed.at[mine, :], received.at[mine, :], own_sem)
    own.start()

    stencil_phase(cells, coef_ref, nb_ref, total_ref, sten_h, sten_l)

    for j in range(tiles):
        lanes = slice(j * LANES, (j + 1) * LANES)
        rates[pl.ds(j, levels, stride=tiles), :] = kd_ref[:, lanes]
        rates[pl.ds(levels * tiles + j, levels, stride=tiles), :] = kv_ref[:, lanes]
    active8 = act8_ref[...]
    bound8 = bl8_ref[...]

    def one_level(i, below):
        level = levels - 1 - i
        is_open = (active8 > level) & (level >= 1)
        inside = bound8 > level
        after = []
        for c in range(2):
            at = pl.ds(pl.multiple_of((c * levels + level) * tiles, 8), tiles)
            face = jnp.where(is_open, jnp.where(inside, rates[at, :], 0.05), 0.0)
            inverse = 1.0 / (1.0 + face + below[c])
            ratio = face * inverse
            recip[at, :] = inverse
            e_ref[at, :] = ratio
            after.append(face - face * ratio)
        return tuple(after)

    nothing = jnp.zeros((tiles, LANES), F32)
    lax.fori_loop(0, levels, one_level, (nothing, nothing), unroll=4)
    for c in range(2):
        r0_ref[c * tiles : (c + 1) * tiles, :] = recip[pl.ds(c * levels * tiles, tiles), :]

    def advance(step, side, g):
        halo_copy(step, 1 - side, g).wait_recv()
        lanes = pl.ds(pl.multiple_of(side * (HW + cells), HW), HW)
        for f in (2 * g, 2 * g + 1):
            put_split(f, lanes, halo[step, side, f])
        source = q_ref if step == 0 else q1
        at = g * 2 * group_rows
        for k in range(HW // BLOCK):
            b = side * (HW // BLOCK) + k
            cols = pl.ds(pl.multiple_of(b * BLOCK, BLOCK), BLOCK)
            window = pl.ds(pl.multiple_of(b * BLOCK, BLOCK), BAND)
            both = jnp.dot(
                split[pl.ds(at, 2 * group_rows), window], sten_h[b], preferred_element_type=F32
            )
            extra = jnp.dot(
                split[pl.ds(at, group_rows), window], sten_l[b], preferred_element_type=F32
            )
            inflow = both[:group_rows] + both[group_rows:] + extra
            live = iota((levels, BLOCK), 0) < act_ref[:, cols]
            for f in (2 * g, 2 * g + 1):
                centre = source[f, :, cols]
                moved = (
                    centre
                    + inflow[(f % 2) * levels : (f % 2 + 1) * levels]
                    - centre * total_ref[0:1, cols]
                )
                moved = jnp.where(live, moved, centre)
                if step == 0:
                    q1[f, :, cols] = moved
                else:
                    for h in range(BLOCK // LANES):
                        z_ref[
                            pl.ds(f * levels * tiles + b * (BLOCK // LANES) + h, levels, stride=tiles), :
                        ] = moved[:, h * LANES : (h + 1) * LANES]
        if step == 0:
            halo_copy(1, side, g).start()

    for side in (near, far):
        for g in range(2):
            advance(0, side, g)
    for f in range(NFIELD):
        put_split(f, pl.ds(HW, cells), q1[f])

    own.wait()
    everyone = pl.ds(0, (n - 1) * USED)
    arrived = pltpu.make_async_remote_copy(
        src_ref=packed.at[everyone, :],
        dst_ref=received.at[everyone, :],
        send_sem=slab_send,
        recv_sem=slab_recv,
        device_id=ident(lax.rem(me + 1, n)),
        device_id_type=MESH,
    )
    arrived.wait_recv()
    scatter_phase(n, received, surface_acc, 8)
    half = NFIELD * tiles
    surface_ref[...] = surface_acc[:half, :] + surface_acc[half:, :]

    for side in (near, far):
        for g in range(2):
            advance(1, side, g)

    def lift(i, above):
        level = levels - 1 - i
        after = []
        for f in range(NFIELD):
            at = pl.ds(pl.multiple_of((f * levels + level) * tiles, 8), tiles)
            own_at = pl.ds(pl.multiple_of((f // 2 * levels + level) * tiles, 8), tiles)
            right_side = z_ref[at, :] + above[f]
            z_ref[at, :] = recip[own_at, :] * right_side
            after.append(e_ref[own_at, :] * right_side)
        return tuple(after)

    lax.fori_loop(0, levels, lift, (nothing,) * NFIELD, unroll=4)
    arrived.wait_send()
    for step in range(ADV_STEPS):
        for side in range(2):
            for g in range(2):
                halo_copy(step, side, g).wait_send()


def finish_kernel(levels, cells, z_ref, e_ref, r0_ref, flux_ref, out_ref, surface_ref, state):
    tiles = cells // LANES
    below = []
    for f in range(NFIELD):
        surface = flux_ref[f * tiles : (f + 1) * tiles, :]
        for a in range(tiles):
            surface_ref[f : f + 1, a * LANES : (a + 1) * LANES] = surface[a : a + 1, :]
        c = f // 2
        top = z_ref[pl.ds(f * levels * tiles, tiles), :] + surface * r0_ref[c * tiles : (c + 1) * tiles, :]
        state[pl.ds(f * levels * tiles, tiles), :] = top
        below.append(top)

    def drop(level, above):
        after = []
        for f in range(NFIELD):
            at = pl.ds(pl.multiple_of((f * levels + level) * tiles, 8), tiles)
            own_at = pl.ds(pl.multiple_of((f // 2 * levels + level) * tiles, 8), tiles)
            value = z_ref[at, :] + e_ref[own_at, :] * above[f]
            state[at, :] = value
            after.append(value)
        return tuple(after)

    lax.fori_loop(1, levels, drop, tuple(below), unroll=4)
    for f in range(NFIELD):
        for j in range(tiles):
            out_ref[f, :, j * LANES : (j + 1) * LANES] = state[
                pl.ds(f * levels * tiles + j, levels, stride=tiles), :
            ]


def vmem(count):
    return [pl.BlockSpec(memory_space=pltpu.VMEM)] * count


def shaped(*shape):
    return jax.ShapeDtypeStruct(shape, F32)


def per_device(
    n, n_inner,
    ocean_state, adv_coef, neighbours, active_levels, boundary_level, kpp_diff, kpp_visc,
    atm_flux, pair_source, pair_weight, pair_device, pair_cell,
):
    levels, cells = ocean_state.shape[1:]
    tiles = cells // LANES
    pairs = pair_source.shape[0]
    wide = (pairs // LANES, LANES)
    rows_all = NFIELD * levels
    z, e, r0, flux = pl.pallas_call(
        functools.partial(move_kernel, n, n_inner, levels, cells),
        out_shape=(
            shaped(rows_all * tiles, LANES),
            shaped(2 * levels * tiles, LANES),
            shaped(2 * tiles, LANES),
            shaped(NFIELD * tiles, LANES),
        ),
        in_specs=vmem(13),
        out_specs=tuple(vmem(4)),
        scratch_shapes=[
            pltpu.VMEM(wide, F32),
            pltpu.VMEM((5 * n, SLOTS), F32),
            pltpu.VMEM((NFIELD * atm_flux.shape[1] // LANES, 8, LANES), F32),
            pltpu.VMEM((n * SLAB, LANES), F32),
            pltpu.VMEM((n * SLAB, LANES), F32),
            pltpu.VMEM((2 * NFIELD * tiles, LANES), F32),
            pltpu.VMEM((ADV_STEPS, 2, NFIELD, levels, HW), F32),
            pltpu.VMEM((NFIELD, levels, cells), F32),
            pltpu.VMEM((2 * rows_all, cells + 2 * HW), BF16),
            pltpu.VMEM((cells // BLOCK, BAND, BLOCK), BF16),
            pltpu.VMEM((cells // BLOCK, BAND, BLOCK), BF16),
            pltpu.VMEM((2 * levels * tiles, LANES), F32),
            pltpu.VMEM((2 * levels * tiles, LANES), F32),
            pltpu.VMEM((8, cells), F32),
            pltpu.SemaphoreType.DMA((ADV_STEPS, 2, 2)),
            pltpu.SemaphoreType.DMA((ADV_STEPS, 2, 2)),
            pltpu.SemaphoreType.DMA,
            pltpu.SemaphoreType.DMA,
            pltpu.SemaphoreType.DMA,
        ],
        compiler_params=pltpu.CompilerParams(
            vmem_limit_bytes=48 * 1024 * 1024, collective_id=0, has_side_effects=True
        ),
        name="move",
    )(
        pair_device.reshape(wide), pair_source.reshape(wide), pair_cell.reshape(wide),
        pair_weight.reshape(wide), atm_flux,
        ocean_state, adv_coef, neighbours, active_levels.reshape(1, cells),
        active_levels.reshape(tiles, LANES), boundary_level.reshape(tiles, LANES),
        kpp_diff, kpp_visc,
    )
    return pl.pallas_call(
        functools.partial(finish_kernel, levels, cells),
        out_shape=(shaped(NFIELD, levels, cells), shaped(NFIELD, cells)),
        in_specs=vmem(4),
        out_specs=tuple(vmem(2)),
        scratch_shapes=[pltpu.VMEM((rows_all * tiles, LANES), F32)],
        compiler_params=pltpu.CompilerParams(vmem_limit_bytes=32 * 1024 * 1024),
        name="finish",
    )(z, e, r0, flux)


def solution(mesh):
    both = ("grp", "ocn")
    placed = (
        P(None, None, both), P(None, both), P(None, both), P(both), P(both), P(None, both),
        P(None, both), P(None, both), P(both), P(both), P(both, None), P(both),
    )
    n_inner = mesh.shape["ocn"]
    return jax.shard_map(
        functools.partial(per_device, mesh.shape["grp"] * n_inner, n_inner),
        mesh=mesh,
        in_specs=placed,
        out_specs=(P(None, None, both), P(None, both)),
        check_vma=False,
    )
```

```python
import functools

import jax
import jax.numpy as jnp
from jax import lax
from jax.experimental import pallas as pl
from jax.experimental.pallas import tpu as pltpu
from jax.sharding import PartitionSpec as P

NFIELD = 4
NEI = 6
HW = 512
ADV_STEPS = 2
SLOTS = 256
LANES = 128
SLAB = 16
USED = 10
BLOCK = 256
BAND = BLOCK + 2 * HW
MESH = pl.DeviceIdType.MESH
F32 = jnp.float32
BF16 = jnp.bfloat16
I32 = jnp.int32


def iota(shape, dim):
    return lax.broadcasted_iota(I32, shape, dim)


def nt_dot(a, b):
    return lax.dot_general(a, b, (((1,), (1,)), ((), ())), preferred_element_type=F32)


def thick(row, count):
    sixteen = jnp.broadcast_to(row, (16, LANES)).astype(BF16)
    return jnp.broadcast_to(sixteen[None], (count // 16, 16, LANES)).reshape(count, LANES)


def rank_phase(n, dev_ref, ranks, chunk):
    iota_d = iota((n, LANES), 0)
    tri = jnp.where(iota((256, 256), 0) <= iota((256, 256), 1), 1.0, 0.0).astype(BF16)

    def some(i, run):
        at = pl.ds(pl.multiple_of(i * chunk, 8), chunk)
        dest = dev_ref[at, :]
        out = []
        for s in range(0, chunk, 2):
            hit = [iota_d == dest[s + h : s + h + 1, :] for h in range(2)]
            member = jnp.concatenate([jnp.where(m, 1.0, 0.0) for m in hit], axis=1).astype(BF16)
            count = jnp.dot(member, tri, preferred_element_type=F32)
            for h in range(2):
                upto = count[:, h * LANES : (h + 1) * LANES] + run
                out.append(jnp.sum(jnp.where(hit[h], upto, 0.0), axis=0, keepdims=True) - 1.0)
            run = run + jnp.broadcast_to(count[:, 255:256], (n, LANES))
        ranks[at, :] = jnp.concatenate(out, axis=0)
        return run

    lax.fori_loop(0, dev_ref.shape[0] // chunk, some, jnp.zeros((n, LANES), F32))


def place_phase(n, dev_ref, src_ref, cell_ref, w_ref, ranks, acc, chunk):
    one, zero = jnp.ones((), BF16), jnp.zeros((), BF16)
    iota_d = iota((n, LANES), 0).astype(F32).astype(BF16)
    iota_r = iota((SLOTS, LANES), 0).astype(F32).astype(BF16)
    acc[...] = jnp.zeros_like(acc)

    def some(i, _):
        at = pl.ds(pl.multiple_of(i * chunk, 8), chunk)
        dest = dev_ref[at, :].astype(F32)
        code = src_ref[at, :] * 1024 + cell_ref[at, :]
        weight = w_ref[at, :]
        rank = ranks[at, :]
        high = weight.astype(BF16).astype(F32)
        pieces = [
            (code & 127).astype(F32),
            ((code >> 7) & 127).astype(F32),
            (code >> 14).astype(F32),
            high,
            weight - high,
        ]
        left = [[] for _ in pieces]
        right = []
        for s in range(chunk):
            mask = iota_d == thick(dest[s : s + 1, :], n)
            right.append(jnp.where(iota_r == thick(rank[s : s + 1, :], SLOTS), one, zero))
            for v, piece in enumerate(pieces):
                left[v].append(jnp.where(mask, thick(piece[s : s + 1, :], n), zero))
        lhs = jnp.concatenate([jnp.concatenate(part, axis=1) for part in left], axis=0)
        acc[...] += nt_dot(lhs, jnp.concatenate(right, axis=1))
        return 0

    lax.fori_loop(0, dev_ref.shape[0] // chunk, some, 0)


def gather_phase(n, me, atm_ref, acc, out_ref, tabs, send):
    ntab = atm_ref.shape[1] // LANES
    tiles = 2
    trips = n // (8 * tiles)
    for f in range(NFIELD):
        for r in range(ntab):
            tabs[f * ntab + r] = jnp.broadcast_to(
                atm_ref[f : f + 1, r * LANES : (r + 1) * LANES], (8, LANES)
            )

    def some(i, _):
        turn = lax.rem(i + me // (8 * tiles), trips)
        todo = []
        for u in range(tiles):
            t = turn * tiles + u
            for h in range(2):
                lanes = slice(h * LANES, (h + 1) * LANES)

                def part(v):
                    return acc[pl.ds(pl.multiple_of(v * n + t * 8, 8), 8), lanes]

                code = (part(0) + part(1) * 128.0 + part(2) * 16384.0).astype(I32)
                weight = part(3) + part(4)
                source = code >> 10
                todo.append(
                    (t, h, weight, source & (LANES - 1), source >> 7,
                     [jnp.zeros((8, LANES), F32)] * NFIELD)
                )
                out_ref[pl.ds(t * 8 * SLAB + 8 + h, 8, stride=SLAB), :] = (code & 1023).astype(F32)
        for r in range(ntab):
            for t, h, weight, low, high, values in todo:
                here = high == r
                for f in range(NFIELD):
                    got = jnp.take_along_axis(tabs[f * ntab + r], low, axis=1)
                    values[f] = jnp.where(here, got, values[f])
        for t, h, weight, low, high, values in todo:
            for f in range(NFIELD):
                out_ref[pl.ds(t * 8 * SLAB + f * 2 + h, 8, stride=SLAB), :] = values[f] * weight

        def each(j, _):
            send(turn * 8 * tiles + lax.rem(j + me, 8 * tiles))
            return 0

        lax.fori_loop(0, 8 * tiles, each, 0)
        return 0

    lax.fori_loop(0, trips, some, 0)


def scatter_phase(n, recv_ref, acc, group):
    one, zero = jnp.ones((), BF16), jnp.zeros((), BF16)
    acc[...] = jnp.zeros_like(acc)
    iota_a = (iota((16, LANES), 0) & 7).astype(F32).astype(BF16)
    iota_b = iota((LANES, LANES), 0).astype(F32).astype(BF16)

    def some(i, _):
        left = [[] for _ in range(4)]
        right = []
        for s in range(group):
            base = pl.multiple_of((i * group + s) * SLAB, 8)
            values = recv_ref[pl.ds(base, 8), :]
            cell = recv_ref[pl.ds(base + 8, 8), :].astype(I32)
            high = values.astype(BF16).astype(F32)
            low = values - high
            major = (cell >> 7).astype(F32)
            minor = (cell & 127).astype(F32)
            for h in range(2):
                hit = iota_a == jnp.broadcast_to(major[h : h + 1, :], (16, LANES)).astype(BF16)
                right.append(jnp.where(iota_b == thick(minor[h : h + 1, :], LANES), one, zero))
                for p, piece in enumerate((high, low)):
                    for g in range(2):
                        pair = jnp.concatenate(
                            [
                                jnp.broadcast_to(piece[f * 2 + h : f * 2 + h + 1, :], (8, LANES))
                                for f in (2 * g, 2 * g + 1)
                            ],
                            axis=0,
                        ).astype(BF16)
                        left[p * 2 + g].append(jnp.where(hit, pair, zero))
        lhs = jnp.concatenate([jnp.concatenate(part, axis=1) for part in left], axis=0)
        acc[...] += nt_dot(lhs, jnp.concatenate(right, axis=1))
        return 0

    lax.fori_loop(0, n // group, some, 0)


def stencil_phase(cells, coef_ref, nb_ref, total_ref, sten_h, sten_l):
    offset = [nb_ref[k : k + 1, :] for k in range(NEI)]
    weight = [coef_ref[k : k + 1, :] for k in range(NEI)]
    total = weight[0]
    for k in range(1, NEI):
        total = total + weight[k]
    total_ref[0:1, :] = total
    merged = []
    for k in range(NEI):
        w = weight[k]
        for j in range(k):
            w = w + jnp.where(offset[j] == offset[k], weight[j], 0.0)
        merged.append(w)
    local = lax.rem(iota((1, cells), 1), BLOCK) + HW
    target = [local + offset[k] for k in range(NEI)]
    for b in range(cells // BLOCK):
        cols = slice(b * BLOCK, (b + 1) * BLOCK)
        aim = [t[:, cols] for t in target]
        put = [w[:, cols] for w in merged]

        def one_band(i, _):
            at = pl.ds(pl.multiple_of(i * 128, 128), 128)
            row = iota((128, BLOCK), 0) + i * 128
            value = jnp.zeros((128, BLOCK), F32)
            for k in range(NEI):
                value = jnp.where(row == aim[k], put[k], value)
            high = value.astype(BF16)
            sten_h[b, at, :] = high
            sten_l[b, at, :] = (value - high.astype(F32)).astype(BF16)
            return 0

        lax.fori_loop(0, BAND // 128, one_band, 0)


def move_kernel(
    n, n_inner, levels, cells,
    dev_hbm, src_hbm, cell_hbm, w_hbm, atm_hbm,
    q_hbm, coef_hbm, nb_hbm, act_hbm, act8_hbm, bl8_hbm, kd_hbm, kv_hbm,
    out_ref, surface_ref,
    z_ref, e_ref, out_vmem,
    dev_ref, src_ref, cell_ref, w_ref, atm_ref,
    q_ref, coef_ref, nb_ref, act_ref, act8_ref, bl8_ref, kd_ref, kv_ref,
    ranks, slots, tabs, packed, received, surface_acc,
    halo, q1, split, sten_h, sten_l, rates, recip, total_ref,
    halo_send, halo_recv, slab_send, slab_recv, own_sem, load_sem, out_sem,
):
    tiles = cells // LANES
    me = lax.axis_index("grp") * n_inner + lax.axis_index("ocn")
    group_rows = NFIELD // 2 * levels

    def ident(d):
        return (d // n_inner, lax.rem(d, n_inner))

    barrier = pltpu.get_barrier_semaphore()

    def greet(i, _):
        pl.semaphore_signal(
            barrier, inc=1, device_id=ident(lax.rem(me + i, n)), device_id_type=MESH
        )
        return 0

    loads = [
        pltpu.make_async_copy(source, target, load_sem.at[i])
        for i, (source, target) in enumerate(
            [
                (dev_hbm, dev_ref), (q_hbm, q_ref), (src_hbm, src_ref), (cell_hbm, cell_ref),
                (w_hbm, w_ref), (atm_hbm, atm_ref), (coef_hbm, coef_ref), (nb_hbm, nb_ref),
                (act_hbm, act_ref), (act8_hbm, act8_ref), (bl8_hbm, bl8_ref), (kd_hbm, kd_ref),
                (kv_hbm, kv_ref),
            ]
        )
    ]
    for load in loads:
        load.start()
    lax.fori_loop(1, n, greet, 0, unroll=8)
    loads[0].wait()
    rank_phase(n, dev_ref, ranks, 32)

    def put_split(f, lanes, value):
        g = f // 2
        at = g * 2 * group_rows + (f % 2) * levels
        high = value.astype(BF16)
        split[pl.ds(at, levels), lanes] = high
        split[pl.ds(at + group_rows, levels), lanes] = (value - high.astype(F32)).astype(BF16)

    loads[1].wait()
    for f in range(NFIELD):
        put_split(f, pl.ds(HW, cells), q_ref[f])
    pl.semaphore_wait(barrier, n - 1)

    far = lax.rem(me, 2)
    near = 1 - far

    def halo_copy(step, side, g):
        source = q_ref if step == 0 else q1
        fields = pl.ds(2 * g, 2)
        return pltpu.make_async_remote_copy(
            src_ref=source.at[fields, :, pl.ds(pl.multiple_of(side * HW, HW), HW)],
            dst_ref=halo.at[step, 1 - side, fields],
            send_sem=halo_send.at[step, side, g],
            recv_sem=halo_recv.at[step, 1 - side, g],
            device_id=ident(lax.rem(me + n - 1 + 2 * side, n)),
            device_id_type=MESH,
        )

    for side in (far, near):
        for g in range(2):
            halo_copy(0, side, g).start()
    for load in loads[2:]:
        load.wait()
    place_phase(n, dev_ref, src_ref, cell_ref, w_ref, ranks, slots, 32)

    def slab_copy(d):
        return pltpu.make_async_remote_copy(
            src_ref=packed.at[pl.ds(pl.multiple_of(d * SLAB, 8), USED), :],
            dst_ref=received.at[pl.ds(pl.multiple_of(me * SLAB, 8), USED), :],
            send_sem=slab_send,
            recv_sem=slab_recv,
            device_id=ident(d),
            device_id_type=MESH,
        )

    def send_slab(d):
        @pl.when(d != me)
        def _():
            slab_copy(d).start()

    gather_phase(n, me, atm_ref, slots, packed, tabs, send_slab)
    mine = pl.ds(pl.multiple_of(me * SLAB, 8), SLAB)
    own = pltpu.make_async_copy(packed.at[mine, :], received.at[mine, :], own_sem)
    own.start()

    stencil_phase(cells, coef_ref, nb_ref, total_ref, sten_h, sten_l)

    def advance(step, side, g):
        halo_copy(step, 1 - side, g).wait_recv()
        lanes = pl.ds(pl.multiple_of(side * (HW + cells), HW), HW)
        for f in (2 * g, 2 * g + 1):
            put_split(f, lanes, halo[step, side, f])
        source = q_ref if step == 0 else q1
        at = g * 2 * group_rows
        for k in range(HW // BLOCK):
            b = side * (HW // BLOCK) + k
            cols = pl.ds(pl.multiple_of(b * BLOCK, BLOCK), BLOCK)
            window = pl.ds(pl.multiple_of(b * BLOCK, BLOCK), BAND)
            both = jnp.dot(
                split[pl.ds(at, 2 * group_rows), window], sten_h[b], preferred_element_type=F32
            )
            extra = jnp.dot(
                split[pl.ds(at, group_rows), window], sten_l[b], preferred_element_type=F32
            )
            inflow = both[:group_rows] + both[group_rows:] + extra
            live = iota((levels, BLOCK), 0) < act_ref[:, cols]
            for f in (2 * g, 2 * g + 1):
                centre = source[f, :, cols]
                moved = (
                    centre
                    + inflow[(f % 2) * levels : (f % 2 + 1) * levels]
                    - centre * total_ref[0:1, cols]
                )
                moved = jnp.where(live, moved, centre)
                if step == 0:
                    q1[f, :, cols] = moved
                else:
                    for h in range(BLOCK // LANES):
                        z_ref[
                            pl.ds(f * levels * tiles + b * (BLOCK // LANES) + h, levels, stride=tiles), :
                        ] = moved[:, h * LANES : (h + 1) * LANES]
        if step == 0:
            halo_copy(1, side, g).start()

    for side in (near, far):
        for g in range(2):
            advance(0, side, g)
    for f in range(NFIELD):
        put_split(f, pl.ds(HW, cells), q1[f])

    for j in range(tiles):
        lanes = slice(j * LANES, (j + 1) * LANES)
        rates[pl.ds(j, levels, stride=tiles), :] = kd_ref[:, lanes]
        rates[pl.ds(levels * tiles + j, levels, stride=tiles), :] = kv_ref[:, lanes]
    active8 = act8_ref[...]
    bound8 = bl8_ref[...]

    def one_level(i, below):
        level = levels - 1 - i
        is_open = (active8 > level) & (level >= 1)
        inside = bound8 > level
        after = []
        for c in range(2):
            at = pl.ds(pl.multiple_of((c * levels + level) * tiles, 8), tiles)
            face = jnp.where(is_open, jnp.where(inside, rates[at, :], 0.05), 0.0)
            inverse = 1.0 / (1.0 + face + below[c])
            ratio = face * inverse
            recip[at, :] = inverse
            e_ref[at, :] = ratio
            after.append(face - face * ratio)
        return tuple(after)

    nothing = jnp.zeros((tiles, LANES), F32)
    lax.fori_loop(0, levels, one_level, (nothing, nothing), unroll=4)

    for g in range(2):
        advance(1, near, g)

    own.wait()
    everyone = pl.ds(0, (n - 1) * USED)
    arrived = pltpu.make_async_remote_copy(
        src_ref=packed.at[everyone, :],
        dst_ref=received.at[everyone, :],
        send_sem=slab_send,
        recv_sem=slab_recv,
        device_id=ident(lax.rem(me + 1, n)),
        device_id_type=MESH,
    )
    arrived.wait_recv()
    scatter_phase(n, received, surface_acc, 16)
    half = NFIELD * tiles
    surface = surface_acc[:half, :] + surface_acc[half:, :]
    surface_acc[:half, :] = surface
    for f in range(NFIELD):
        for a in range(tiles):
            r = f * tiles + a
            surface_ref[f : f + 1, a * LANES : (a + 1) * LANES] = surface[r : r + 1, :]


    def out_copy(g):
        fields = pl.ds(2 * g, 2)
        return pltpu.make_async_copy(out_vmem.at[fields], out_ref.at[fields], out_sem.at[g])

    for g in range(2):
        advance(1, far, g)
        fields = (2 * g, 2 * g + 1)

        def lift(i, above):
            level = levels - 1 - i
            own_at = pl.ds(pl.multiple_of((g * levels + level) * tiles, 8), tiles)
            after = []
            for f, carried in zip(fields, above):
                at = pl.ds(pl.multiple_of((f * levels + level) * tiles, 8), tiles)
                right_side = z_ref[at, :] + carried
                z_ref[at, :] = recip[own_at, :] * right_side
                after.append(e_ref[own_at, :] * right_side)
            return tuple(after)

        lax.fori_loop(0, levels, lift, (nothing,) * 2, unroll=8)
        below = []
        for f in fields:
            at = pl.ds(f * levels * tiles, tiles)
            flux = surface_acc[f * tiles : (f + 1) * tiles, :]
            top = z_ref[at, :] + flux * recip[pl.ds(g * levels * tiles, tiles), :]
            z_ref[at, :] = top
            below.append(top)

        def drop(level, above):
            own_at = pl.ds(pl.multiple_of((g * levels + level) * tiles, 8), tiles)
            after = []
            for f, carried in zip(fields, above):
                at = pl.ds(pl.multiple_of((f * levels + level) * tiles, 8), tiles)
                value = z_ref[at, :] + e_ref[own_at, :] * carried
                z_ref[at, :] = value
                after.append(value)
            return tuple(after)

        lax.fori_loop(1, levels, drop, tuple(below), unroll=8)
        for f in fields:
            for j in range(tiles):
                out_vmem[f, :, j * LANES : (j + 1) * LANES] = z_ref[
                    pl.ds(f * levels * tiles + j, levels, stride=tiles), :
                ]
        out_copy(g).start()
    for g in range(2):
        out_copy(g).wait()
    arrived.wait_send()
    for step in range(ADV_STEPS):
        for side in range(2):
            for g in range(2):
                halo_copy(step, side, g).wait_send()


def vmem(count):
    return [pl.BlockSpec(memory_space=pltpu.VMEM)] * count


def shaped(*shape):
    return jax.ShapeDtypeStruct(shape, F32)


def per_device(
    n, n_inner,
    ocean_state, adv_coef, neighbours, active_levels, boundary_level, kpp_diff, kpp_visc,
    atm_flux, pair_source, pair_weight, pair_device, pair_cell,
):
    levels, cells = ocean_state.shape[1:]
    tiles = cells // LANES
    pairs = pair_source.shape[0]
    wide = (pairs // LANES, LANES)
    rows_all = NFIELD * levels
    return pl.pallas_call(
        functools.partial(move_kernel, n, n_inner, levels, cells),
        out_shape=(shaped(NFIELD, levels, cells), shaped(NFIELD, cells)),
        in_specs=[pl.BlockSpec(memory_space=pltpu.HBM)] * 13,
        out_specs=(pl.BlockSpec(memory_space=pltpu.HBM), vmem(1)[0]),
        scratch_shapes=[
            pltpu.VMEM((rows_all * tiles, LANES), F32),
            pltpu.VMEM((2 * levels * tiles, LANES), F32),
            pltpu.VMEM((NFIELD, levels, cells), F32),
            pltpu.VMEM(wide, I32),
            pltpu.VMEM(wide, I32),
            pltpu.VMEM(wide, I32),
            pltpu.VMEM(wide, F32),
            pltpu.VMEM(atm_flux.shape, F32),
            pltpu.VMEM((NFIELD, levels, cells), F32),
            pltpu.VMEM((NEI, cells), F32),
            pltpu.VMEM((NEI, cells), I32),
            pltpu.VMEM((1, cells), I32),
            pltpu.VMEM((tiles, LANES), I32),
            pltpu.VMEM((tiles, LANES), I32),
            pltpu.VMEM((levels, cells), F32),
            pltpu.VMEM((levels, cells), F32),
            pltpu.VMEM(wide, F32),
            pltpu.VMEM((5 * n, SLOTS), F32),
            pltpu.VMEM((NFIELD * atm_flux.shape[1] // LANES, 8, LANES), F32),
            pltpu.VMEM((n * SLAB, LANES), F32),
            pltpu.VMEM((n * SLAB, LANES), F32),
            pltpu.VMEM((2 * NFIELD * tiles, LANES), F32),
            pltpu.VMEM((ADV_STEPS, 2, NFIELD, levels, HW), F32),
            pltpu.VMEM((NFIELD, levels, cells), F32),
            pltpu.VMEM((2 * rows_all, cells + 2 * HW), BF16),
            pltpu.VMEM((cells // BLOCK, BAND, BLOCK), BF16),
            pltpu.VMEM((cells // BLOCK, BAND, BLOCK), BF16),
            pltpu.VMEM((2 * levels * tiles, LANES), F32),
            pltpu.VMEM((2 * levels * tiles, LANES), F32),
            pltpu.VMEM((8, cells), F32),
            pltpu.SemaphoreType.DMA((ADV_STEPS, 2, 2)),
            pltpu.SemaphoreType.DMA((ADV_STEPS, 2, 2)),
            pltpu.SemaphoreType.DMA,
            pltpu.SemaphoreType.DMA,
            pltpu.SemaphoreType.DMA,
            pltpu.SemaphoreType.DMA((13,)),
            pltpu.SemaphoreType.DMA((2,)),
        ],
        compiler_params=pltpu.CompilerParams(
            vmem_limit_bytes=63 * 1024 * 1024, collective_id=0, has_side_effects=True
        ),
        name="move",
    )(
        pair_device.reshape(wide), pair_source.reshape(wide), pair_cell.reshape(wide),
        pair_weight.reshape(wide), atm_flux,
        ocean_state, adv_coef, neighbours, active_levels.reshape(1, cells),
        active_levels.reshape(tiles, LANES), boundary_level.reshape(tiles, LANES),
        kpp_diff, kpp_visc,
    )


def solution(mesh):
    both = ("grp", "ocn")
    placed = (
        P(None, None, both), P(None, both), P(None, both), P(both), P(both), P(None, both),
        P(None, both), P(None, both), P(both), P(both), P(both, None), P(both),
    )
    n_inner = mesh.shape["ocn"]
    return jax.shard_map(
        functools.partial(per_device, mesh.shape["grp"] * n_inner, n_inner),
        mesh=mesh,
        in_specs=placed,
        out_specs=(P(None, None, both), P(None, both)),
        check_vma=False,
    )
```

```python
import functools

import jax
import jax.numpy as jnp
from jax import lax
from jax.experimental import pallas as pl
from jax.experimental.pallas import tpu as pltpu
from jax.sharding import PartitionSpec as P

NFIELD = 4
NEI = 6
HW = 512
ADV_STEPS = 2
SLOTS = 256
LANES = 128
SLAB = 16
USED = 10
BLOCK = 256
BAND = BLOCK + 2 * HW
MESH = pl.DeviceIdType.MESH
F32 = jnp.float32
BF16 = jnp.bfloat16
I32 = jnp.int32


def iota(shape, dim):
    return lax.broadcasted_iota(I32, shape, dim)


def nt_dot(a, b):
    return lax.dot_general(a, b, (((1,), (1,)), ((), ())), preferred_element_type=F32)


def thick(row, count):
    sixteen = jnp.broadcast_to(row, (16, LANES)).astype(BF16)
    return jnp.broadcast_to(sixteen[None], (count // 16, 16, LANES)).reshape(count, LANES)


def rank_phase(n, dev_ref, ranks, chunk):
    iota_d = iota((n, LANES), 0)
    tri = jnp.where(iota((256, 256), 0) <= iota((256, 256), 1), 1.0, 0.0).astype(BF16)

    def some(i, run):
        at = pl.ds(pl.multiple_of(i * chunk, 8), chunk)
        dest = dev_ref[at, :]
        out = []
        for s in range(0, chunk, 2):
            hit = [iota_d == dest[s + h : s + h + 1, :] for h in range(2)]
            member = jnp.concatenate([jnp.where(m, 1.0, 0.0) for m in hit], axis=1).astype(BF16)
            count = jnp.dot(member, tri, preferred_element_type=F32)
            for h in range(2):
                upto = count[:, h * LANES : (h + 1) * LANES] + run
                out.append(jnp.sum(jnp.where(hit[h], upto, 0.0), axis=0, keepdims=True) - 1.0)
            run = run + jnp.broadcast_to(count[:, 255:256], (n, LANES))
        ranks[at, :] = jnp.concatenate(out, axis=0)
        return run

    lax.fori_loop(0, dev_ref.shape[0] // chunk, some, jnp.zeros((n, LANES), F32))


def place_phase(n, dev_ref, src_ref, cell_ref, w_ref, ranks, acc, chunk):
    one, zero = jnp.ones((), BF16), jnp.zeros((), BF16)
    iota_d = iota((n, LANES), 0).astype(F32).astype(BF16)
    iota_r = iota((SLOTS, LANES), 0).astype(F32).astype(BF16)
    acc[...] = jnp.zeros_like(acc)

    def some(i, _):
        at = pl.ds(pl.multiple_of(i * chunk, 8), chunk)
        dest = dev_ref[at, :].astype(F32)
        code = src_ref[at, :] * 1024 + cell_ref[at, :]
        weight = w_ref[at, :]
        rank = ranks[at, :]
        high = weight.astype(BF16).astype(F32)
        pieces = [
            (code & 127).astype(F32),
            ((code >> 7) & 127).astype(F32),
            (code >> 14).astype(F32),
            high,
            weight - high,
        ]
        left = [[] for _ in pieces]
        right = []
        for s in range(chunk):
            mask = iota_d == thick(dest[s : s + 1, :], n)
            right.append(jnp.where(iota_r == thick(rank[s : s + 1, :], SLOTS), one, zero))
            for v, piece in enumerate(pieces):
                left[v].append(jnp.where(mask, thick(piece[s : s + 1, :], n), zero))
        lhs = jnp.concatenate([jnp.concatenate(part, axis=1) for part in left], axis=0)
        acc[...] += nt_dot(lhs, jnp.concatenate(right, axis=1))
        return 0

    lax.fori_loop(0, dev_ref.shape[0] // chunk, some, 0)


def gather_phase(n, n_inner, me, atm_ref, acc, out_ref, tabs, send):
    ntab = atm_ref.shape[1] // LANES
    tiles = 2
    trips = n // (8 * tiles)
    outer = n // n_inner
    inner = n_inner // 8
    for f in range(NFIELD):
        for r in range(ntab):
            tabs[f * ntab + r] = jnp.broadcast_to(
                atm_ref[f : f + 1, r * LANES : (r + 1) * LANES], (8, LANES)
            )

    def some(i, _):
        todo = []
        turns = []
        for u in range(tiles):
            m = i * tiles + u
            up = lax.rem(m, outer)
            across = m // outer + inner // 2 * lax.rem(up, 2) + up // 2
            t = lax.rem(me // n_inner + up, outer) * inner + lax.rem(
                lax.rem(me, n_inner) // 8 + across, inner
            )
            turns.append(t)
            for h in range(2):
                lanes = slice(h * LANES, (h + 1) * LANES)

                def part(v):
                    return acc[pl.ds(pl.multiple_of(v * n + t * 8, 8), 8), lanes]

                code = (part(0) + part(1) * 128.0 + part(2) * 16384.0).astype(I32)
                weight = part(3) + part(4)
                source = code >> 10
                todo.append(
                    (t, h, weight, source & (LANES - 1), source >> 7,
                     [jnp.zeros((8, LANES), F32)] * NFIELD)
                )
                out_ref[pl.ds(t * 8 * SLAB + 8 + h, 8, stride=SLAB), :] = (code & 1023).astype(F32)
        for r in range(ntab):
            for t, h, weight, low, high, values in todo:
                here = high == r
                for f in range(NFIELD):
                    got = jnp.take_along_axis(tabs[f * ntab + r], low, axis=1)
                    values[f] = jnp.where(here, got, values[f])
        for t, h, weight, low, high, values in todo:
            for f in range(NFIELD):
                out_ref[pl.ds(t * 8 * SLAB + f * 2 + h, 8, stride=SLAB), :] = values[f] * weight

        def each(j, _):
            for t in turns:
                send(t * 8 + lax.rem(j + me, 8))
            return 0

        lax.fori_loop(0, 8, each, 0)
        return 0

    lax.fori_loop(0, trips, some, 0)


def scatter_phase(n, recv_ref, acc, group):
    one, zero = jnp.ones((), BF16), jnp.zeros((), BF16)
    acc[...] = jnp.zeros_like(acc)
    iota_a = (iota((16, LANES), 0) & 7).astype(F32).astype(BF16)
    iota_b = iota((LANES, LANES), 0).astype(F32).astype(BF16)

    def some(i, _):
        left = [[] for _ in range(4)]
        right = []
        for s in range(group):
            base = pl.multiple_of((i * group + s) * SLAB, 8)
            values = recv_ref[pl.ds(base, 8), :]
            cell = recv_ref[pl.ds(base + 8, 8), :].astype(I32)
            high = values.astype(BF16).astype(F32)
            low = values - high
            major = (cell >> 7).astype(F32)
            minor = (cell & 127).astype(F32)
            for h in range(2):
                hit = iota_a == jnp.broadcast_to(major[h : h + 1, :], (16, LANES)).astype(BF16)
                right.append(jnp.where(iota_b == thick(minor[h : h + 1, :], LANES), one, zero))
                for p, piece in enumerate((high, low)):
                    for g in range(2):
                        pair = jnp.concatenate(
                            [
                                jnp.broadcast_to(piece[f * 2 + h : f * 2 + h + 1, :], (8, LANES))
                                for f in (2 * g, 2 * g + 1)
                            ],
                            axis=0,
                        ).astype(BF16)
                        left[p * 2 + g].append(jnp.where(hit, pair, zero))
        lhs = jnp.concatenate([jnp.concatenate(part, axis=1) for part in left], axis=0)
        acc[...] += nt_dot(lhs, jnp.concatenate(right, axis=1))
        return 0

    lax.fori_loop(0, n // group, some, 0)


def stencil_phase(cells, coef_ref, nb_ref, total_ref, sten_h, sten_l):
    offset = [nb_ref[k : k + 1, :] for k in range(NEI)]
    weight = [coef_ref[k : k + 1, :] for k in range(NEI)]
    total = weight[0]
    for k in range(1, NEI):
        total = total + weight[k]
    total_ref[0:1, :] = total
    merged = []
    for k in range(NEI):
        w = weight[k]
        for j in range(k):
            w = w + jnp.where(offset[j] == offset[k], weight[j], 0.0)
        merged.append(w)
    local = lax.rem(iota((1, cells), 1), BLOCK) + HW
    target = [local + offset[k] for k in range(NEI)]
    for b in range(cells // BLOCK):
        cols = slice(b * BLOCK, (b + 1) * BLOCK)
        aim = [t[:, cols] for t in target]
        put = [w[:, cols] for w in merged]

        def one_band(i, _):
            at = pl.ds(pl.multiple_of(i * 128, 128), 128)
            row = iota((128, BLOCK), 0) + i * 128
            value = jnp.zeros((128, BLOCK), F32)
            for k in range(NEI):
                value = jnp.where(row == aim[k], put[k], value)
            high = value.astype(BF16)
            sten_h[b, at, :] = high
            sten_l[b, at, :] = (value - high.astype(F32)).astype(BF16)
            return 0

        lax.fori_loop(0, BAND // 128, one_band, 0)


def move_kernel(
    n, n_inner, levels, cells,
    dev_hbm, src_hbm, cell_hbm, w_hbm, atm_hbm,
    q_hbm, coef_hbm, nb_hbm, act_hbm, act8_hbm, bl8_hbm, kd_hbm, kv_hbm,
    out_ref, surface_ref,
    z_ref, e_ref, out_vmem,
    dev_ref, src_ref, cell_ref, w_ref, atm_ref,
    q_ref, coef_ref, nb_ref, act_ref, act8_ref, bl8_ref, kd_ref, kv_ref,
    ranks, slots, tabs, packed, received, surface_acc,
    halo, q1, split, sten_h, sten_l, rates, recip, total_ref,
    halo_send, halo_recv, slab_send, slab_recv, own_sem, load_sem, out_sem,
):
    tiles = cells // LANES
    me = lax.axis_index("grp") * n_inner + lax.axis_index("ocn")
    group_rows = NFIELD // 2 * levels

    def ident(d):
        return (d // n_inner, lax.rem(d, n_inner))

    barrier = pltpu.get_barrier_semaphore()

    my_outer = lax.axis_index("grp")
    my_inner = lax.axis_index("ocn")

    def greet(i, _):
        for g in range(n // n_inner):
            other = (lax.rem(my_outer + g, n // n_inner), lax.rem(my_inner + i, n_inner))

            def hello():
                pl.semaphore_signal(barrier, inc=1, device_id=other, device_id_type=MESH)

            if g == 0:
                pl.when(i != 0)(hello)
            else:
                hello()
        return 0

    loads = [
        pltpu.make_async_copy(source, target, load_sem.at[i])
        for i, (source, target) in enumerate(
            [
                (dev_hbm, dev_ref), (q_hbm, q_ref), (src_hbm, src_ref), (cell_hbm, cell_ref),
                (w_hbm, w_ref), (atm_hbm, atm_ref), (coef_hbm, coef_ref), (nb_hbm, nb_ref),
                (act_hbm, act_ref), (act8_hbm, act8_ref), (bl8_hbm, bl8_ref), (kd_hbm, kd_ref),
                (kv_hbm, kv_ref),
            ]
        )
    ]
    for load in loads:
        load.start()
    lax.fori_loop(0, n_inner, greet, 0, unroll=4)
    loads[0].wait()
    rank_phase(n, dev_ref, ranks, 32)

    def put_split(f, lanes, value):
        g = f // 2
        at = g * 2 * group_rows + (f % 2) * levels
        high = value.astype(BF16)
        split[pl.ds(at, levels), lanes] = high
        split[pl.ds(at + group_rows, levels), lanes] = (value - high.astype(F32)).astype(BF16)

    loads[1].wait()
    for f in range(NFIELD):
        put_split(f, pl.ds(HW, cells), q_ref[f])
    pl.semaphore_wait(barrier, n - 1)

    far = lax.rem(me, 2)
    near = 1 - far

    def halo_copy(step, side, g):
        source = q_ref if step == 0 else q1
        fields = pl.ds(2 * g, 2)
        return pltpu.make_async_remote_copy(
            src_ref=source.at[fields, :, pl.ds(pl.multiple_of(side * HW, HW), HW)],
            dst_ref=halo.at[step, 1 - side, fields],
            send_sem=halo_send.at[step, side, g],
            recv_sem=halo_recv.at[step, 1 - side, g],
            device_id=ident(lax.rem(me + n - 1 + 2 * side, n)),
            device_id_type=MESH,
        )

    for side in (far, near):
        for g in range(2):
            halo_copy(0, side, g).start()
    for load in loads[2:]:
        load.wait()
    place_phase(n, dev_ref, src_ref, cell_ref, w_ref, ranks, slots, 32)

    def slab_copy(d):
        return pltpu.make_async_remote_copy(
            src_ref=packed.at[pl.ds(pl.multiple_of(d * SLAB, 8), USED), :],
            dst_ref=received.at[pl.ds(pl.multiple_of(me * SLAB, 8), USED), :],
            send_sem=slab_send,
            recv_sem=slab_recv,
            device_id=ident(d),
            device_id_type=MESH,
        )

    def send_slab(d):
        @pl.when(d != me)
        def _():
            slab_copy(d).start()

    gather_phase(n, n_inner, me, atm_ref, slots, packed, tabs, send_slab)
    mine = pl.ds(pl.multiple_of(me * SLAB, 8), SLAB)
    own = pltpu.make_async_copy(packed.at[mine, :], received.at[mine, :], own_sem)
    own.start()

    stencil_phase(cells, coef_ref, nb_ref, total_ref, sten_h, sten_l)

    def advance(step, side, g):
        halo_copy(step, 1 - side, g).wait_recv()
        lanes = pl.ds(pl.multiple_of(side * (HW + cells), HW), HW)
        for f in (2 * g, 2 * g + 1):
            put_split(f, lanes, halo[step, side, f])
        source = q_ref if step == 0 else q1
        at = g * 2 * group_rows
        for k in range(HW // BLOCK):
            b = side * (HW // BLOCK) + k
            cols = pl.ds(pl.multiple_of(b * BLOCK, BLOCK), BLOCK)
            window = pl.ds(pl.multiple_of(b * BLOCK, BLOCK), BAND)
            both = jnp.dot(
                split[pl.ds(at, 2 * group_rows), window], sten_h[b], preferred_element_type=F32
            )
            extra = jnp.dot(
                split[pl.ds(at, group_rows), window], sten_l[b], preferred_element_type=F32
            )
            inflow = both[:group_rows] + both[group_rows:] + extra
            live = iota((levels, BLOCK), 0) < act_ref[:, cols]
            for f in (2 * g, 2 * g + 1):
                centre = source[f, :, cols]
                moved = (
                    centre
                    + inflow[(f % 2) * levels : (f % 2 + 1) * levels]
                    - centre * total_ref[0:1, cols]
                )
                moved = jnp.where(live, moved, centre)
                if step == 0:
                    q1[f, :, cols] = moved
                else:
                    for h in range(BLOCK // LANES):
                        z_ref[
                            pl.ds(f * levels * tiles + b * (BLOCK // LANES) + h, levels, stride=tiles), :
                        ] = moved[:, h * LANES : (h + 1) * LANES]
        if step == 0:
            halo_copy(1, side, g).start()

    for side in (near, far):
        for g in range(2):
            advance(0, side, g)
    for f in range(NFIELD):
        put_split(f, pl.ds(HW, cells), q1[f])

    for j in range(tiles):
        lanes = slice(j * LANES, (j + 1) * LANES)
        rates[pl.ds(j, levels, stride=tiles), :] = kd_ref[:, lanes]
        rates[pl.ds(levels * tiles + j, levels, stride=tiles), :] = kv_ref[:, lanes]
    active8 = act8_ref[...]
    bound8 = bl8_ref[...]

    def one_level(i, below):
        level = levels - 1 - i
        is_open = (active8 > level) & (level >= 1)
        inside = bound8 > level
        after = []
        for c in range(2):
            at = pl.ds(pl.multiple_of((c * levels + level) * tiles, 8), tiles)
            face = jnp.where(is_open, jnp.where(inside, rates[at, :], 0.05), 0.0)
            inverse = 1.0 / (1.0 + face + below[c])
            ratio = face * inverse
            recip[at, :] = inverse
            e_ref[at, :] = ratio
            after.append(face - face * ratio)
        return tuple(after)

    nothing = jnp.zeros((tiles, LANES), F32)
    lax.fori_loop(0, levels, one_level, (nothing, nothing), unroll=4)

    for g in range(2):
        advance(1, near, g)

    own.wait()
    everyone = pl.ds(0, (n - 1) * USED)
    arrived = pltpu.make_async_remote_copy(
        src_ref=packed.at[everyone, :],
        dst_ref=received.at[everyone, :],
        send_sem=slab_send,
        recv_sem=slab_recv,
        device_id=ident(lax.rem(me + 1, n)),
        device_id_type=MESH,
    )
    arrived.wait_recv()
    scatter_phase(n, received, surface_acc, 16)
    half = NFIELD * tiles
    surface = surface_acc[:half, :] + surface_acc[half:, :]
    surface_acc[:half, :] = surface
    for f in range(NFIELD):
        for a in range(tiles):
            r = f * tiles + a
            surface_ref[f : f + 1, a * LANES : (a + 1) * LANES] = surface[r : r + 1, :]


    def out_copy(g):
        fields = pl.ds(2 * g, 2)
        return pltpu.make_async_copy(out_vmem.at[fields], out_ref.at[fields], out_sem.at[g])

    for g in range(2):
        advance(1, far, g)
        fields = (2 * g, 2 * g + 1)

        def lift(i, above):
            level = levels - 1 - i
            own_at = pl.ds(pl.multiple_of((g * levels + level) * tiles, 8), tiles)
            after = []
            for f, carried in zip(fields, above):
                at = pl.ds(pl.multiple_of((f * levels + level) * tiles, 8), tiles)
                right_side = z_ref[at, :] + carried
                z_ref[at, :] = recip[own_at, :] * right_side
                after.append(e_ref[own_at, :] * right_side)
            return tuple(after)

        lax.fori_loop(0, levels, lift, (nothing,) * 2, unroll=8)
        below = []
        for f in fields:
            at = pl.ds(f * levels * tiles, tiles)
            flux = surface_acc[f * tiles : (f + 1) * tiles, :]
            top = z_ref[at, :] + flux * recip[pl.ds(g * levels * tiles, tiles), :]
            z_ref[at, :] = top
            below.append(top)

        def drop(level, above):
            own_at = pl.ds(pl.multiple_of((g * levels + level) * tiles, 8), tiles)
            after = []
            for f, carried in zip(fields, above):
                at = pl.ds(pl.multiple_of((f * levels + level) * tiles, 8), tiles)
                value = z_ref[at, :] + e_ref[own_at, :] * carried
                z_ref[at, :] = value
                after.append(value)
            return tuple(after)

        lax.fori_loop(1, levels, drop, tuple(below), unroll=8)
        for f in fields:
            for j in range(tiles):
                out_vmem[f, :, j * LANES : (j + 1) * LANES] = z_ref[
                    pl.ds(f * levels * tiles + j, levels, stride=tiles), :
                ]
        out_copy(g).start()
    for g in range(2):
        out_copy(g).wait()
    arrived.wait_send()
    for step in range(ADV_STEPS):
        for side in range(2):
            for g in range(2):
                halo_copy(step, side, g).wait_send()


def vmem(count):
    return [pl.BlockSpec(memory_space=pltpu.VMEM)] * count


def shaped(*shape):
    return jax.ShapeDtypeStruct(shape, F32)


def per_device(
    n, n_inner,
    ocean_state, adv_coef, neighbours, active_levels, boundary_level, kpp_diff, kpp_visc,
    atm_flux, pair_source, pair_weight, pair_device, pair_cell,
):
    levels, cells = ocean_state.shape[1:]
    tiles = cells // LANES
    pairs = pair_source.shape[0]
    wide = (pairs // LANES, LANES)
    rows_all = NFIELD * levels
    return pl.pallas_call(
        functools.partial(move_kernel, n, n_inner, levels, cells),
        out_shape=(shaped(NFIELD, levels, cells), shaped(NFIELD, cells)),
        in_specs=[pl.BlockSpec(memory_space=pltpu.HBM)] * 13,
        out_specs=(pl.BlockSpec(memory_space=pltpu.HBM), vmem(1)[0]),
        scratch_shapes=[
            pltpu.VMEM((rows_all * tiles, LANES), F32),
            pltpu.VMEM((2 * levels * tiles, LANES), F32),
            pltpu.VMEM((NFIELD, levels, cells), F32),
            pltpu.VMEM(wide, I32),
            pltpu.VMEM(wide, I32),
            pltpu.VMEM(wide, I32),
            pltpu.VMEM(wide, F32),
            pltpu.VMEM(atm_flux.shape, F32),
            pltpu.VMEM((NFIELD, levels, cells), F32),
            pltpu.VMEM((NEI, cells), F32),
            pltpu.VMEM((NEI, cells), I32),
            pltpu.VMEM((1, cells), I32),
            pltpu.VMEM((tiles, LANES), I32),
            pltpu.VMEM((tiles, LANES), I32),
            pltpu.VMEM((levels, cells), F32),
            pltpu.VMEM((levels, cells), F32),
            pltpu.VMEM(wide, F32),
            pltpu.VMEM((5 * n, SLOTS), F32),
            pltpu.VMEM((NFIELD * atm_flux.shape[1] // LANES, 8, LANES), F32),
            pltpu.VMEM((n * SLAB, LANES), F32),
            pltpu.VMEM((n * SLAB, LANES), F32),
            pltpu.VMEM((2 * NFIELD * tiles, LANES), F32),
            pltpu.VMEM((ADV_STEPS, 2, NFIELD, levels, HW), F32),
            pltpu.VMEM((NFIELD, levels, cells), F32),
            pltpu.VMEM((2 * rows_all, cells + 2 * HW), BF16),
            pltpu.VMEM((cells // BLOCK, BAND, BLOCK), BF16),
            pltpu.VMEM((cells // BLOCK, BAND, BLOCK), BF16),
            pltpu.VMEM((2 * levels * tiles, LANES), F32),
            pltpu.VMEM((2 * levels * tiles, LANES), F32),
            pltpu.VMEM((8, cells), F32),
            pltpu.SemaphoreType.DMA((ADV_STEPS, 2, 2)),
            pltpu.SemaphoreType.DMA((ADV_STEPS, 2, 2)),
            pltpu.SemaphoreType.DMA,
            pltpu.SemaphoreType.DMA,
            pltpu.SemaphoreType.DMA,
            pltpu.SemaphoreType.DMA((13,)),
            pltpu.SemaphoreType.DMA((2,)),
        ],
        compiler_params=pltpu.CompilerParams(
            vmem_limit_bytes=63 * 1024 * 1024, collective_id=0, has_side_effects=True
        ),
        name="move",
    )(
        pair_device.reshape(wide), pair_source.reshape(wide), pair_cell.reshape(wide),
        pair_weight.reshape(wide), atm_flux,
        ocean_state, adv_coef, neighbours, active_levels.reshape(1, cells),
        active_levels.reshape(tiles, LANES), boundary_level.reshape(tiles, LANES),
        kpp_diff, kpp_visc,
    )


def solution(mesh):
    both = ("grp", "ocn")
    placed = (
        P(None, None, both), P(None, both), P(None, both), P(both), P(both), P(None, both),
        P(None, both), P(None, both), P(both), P(both), P(both, None), P(both),
    )
    n_inner = mesh.shape["ocn"]
    return jax.shard_map(
        functools.partial(per_device, mesh.shape["grp"] * n_inner, n_inner),
        mesh=mesh,
        in_specs=placed,
        out_specs=(P(None, None, both), P(None, both)),
        check_vma=False,
    )
```

```python
import functools

import jax
import jax.numpy as jnp
from jax import lax
from jax.experimental import pallas as pl
from jax.experimental.pallas import tpu as pltpu
from jax.sharding import PartitionSpec as P

NFIELD = 4
NEI = 6
HW = 512
ADV_STEPS = 2
SLOTS = 256
LANES = 128
SLAB = 16
USED = 10
BLOCK = 256
BAND = BLOCK + 2 * HW
MESH = pl.DeviceIdType.MESH
F32 = jnp.float32
BF16 = jnp.bfloat16
I32 = jnp.int32


def iota(shape, dim):
    return lax.broadcasted_iota(I32, shape, dim)


def nt_dot(a, b):
    return lax.dot_general(a, b, (((1,), (1,)), ((), ())), preferred_element_type=F32)


def thick(row, count):
    sixteen = jnp.broadcast_to(row, (16, LANES)).astype(BF16)
    return jnp.broadcast_to(sixteen[None], (count // 16, 16, LANES)).reshape(count, LANES)


def rank_phase(n, dev_ref, ranks, chunk):
    iota_d = iota((n, LANES), 0)
    tri = jnp.where(iota((256, 256), 0) <= iota((256, 256), 1), 1.0, 0.0).astype(BF16)

    def some(i, run):
        at = pl.ds(pl.multiple_of(i * chunk, 8), chunk)
        dest = dev_ref[at, :]
        out = []
        for s in range(0, chunk, 2):
            hit = [iota_d == dest[s + h : s + h + 1, :] for h in range(2)]
            member = jnp.concatenate([jnp.where(m, 1.0, 0.0) for m in hit], axis=1).astype(BF16)
            count = jnp.dot(member, tri, preferred_element_type=F32)
            for h in range(2):
                upto = count[:, h * LANES : (h + 1) * LANES] + run
                out.append(jnp.sum(jnp.where(hit[h], upto, 0.0), axis=0, keepdims=True) - 1.0)
            run = run + jnp.broadcast_to(count[:, 255:256], (n, LANES))
        ranks[at, :] = jnp.concatenate(out, axis=0)
        return run

    lax.fori_loop(0, dev_ref.shape[0] // chunk, some, jnp.zeros((n, LANES), F32))


def place_phase(n, dev_ref, src_ref, cell_ref, w_ref, ranks, acc, chunk):
    one, zero = jnp.ones((), BF16), jnp.zeros((), BF16)
    iota_d = iota((n, LANES), 0).astype(F32).astype(BF16)
    iota_r = iota((SLOTS, LANES), 0).astype(F32).astype(BF16)
    acc[...] = jnp.zeros_like(acc)

    def some(i, _):
        at = pl.ds(pl.multiple_of(i * chunk, 8), chunk)
        dest = dev_ref[at, :].astype(F32)
        code = src_ref[at, :] * 1024 + cell_ref[at, :]
        weight = w_ref[at, :]
        rank = ranks[at, :]
        high = weight.astype(BF16).astype(F32)
        pieces = [
            (code & 127).astype(F32),
            ((code >> 7) & 127).astype(F32),
            (code >> 14).astype(F32),
            high,
            weight - high,
        ]
        left = [[] for _ in pieces]
        right = []
        for s in range(chunk):
            mask = iota_d == thick(dest[s : s + 1, :], n)
            right.append(jnp.where(iota_r == thick(rank[s : s + 1, :], SLOTS), one, zero))
            for v, piece in enumerate(pieces):
                left[v].append(jnp.where(mask, thick(piece[s : s + 1, :], n), zero))
        lhs = jnp.concatenate([jnp.concatenate(part, axis=1) for part in left], axis=0)
        acc[...] += nt_dot(lhs, jnp.concatenate(right, axis=1))
        return 0

    lax.fori_loop(0, dev_ref.shape[0] // chunk, some, 0)


def gather_phase(n, n_inner, me, atm_ref, acc, out_ref, tabs, send):
    ntab = atm_ref.shape[1] // LANES
    tiles = 2
    trips = n // (8 * tiles)
    outer = n // n_inner
    inner = n_inner // 8
    for f in range(NFIELD):
        for r in range(ntab):
            tabs[f * ntab + r] = jnp.broadcast_to(
                atm_ref[f : f + 1, r * LANES : (r + 1) * LANES], (8, LANES)
            )

    def some(i, _):
        todo = []
        turns = []
        for u in range(tiles):
            m = i * tiles + u
            up = lax.rem(m, outer)
            across = m // outer + inner // 2 * lax.rem(up, 2) + up // 2
            t = lax.rem(me // n_inner + up, outer) * inner + lax.rem(
                lax.rem(me, n_inner) // 8 + across, inner
            )
            turns.append(t)
            for h in range(2):
                lanes = slice(h * LANES, (h + 1) * LANES)

                def part(v):
                    return acc[pl.ds(pl.multiple_of(v * n + t * 8, 8), 8), lanes]

                code = (part(0) + part(1) * 128.0 + part(2) * 16384.0).astype(I32)
                weight = part(3) + part(4)
                source = code >> 10
                todo.append(
                    (t, h, weight, source & (LANES - 1), source >> 7,
                     [jnp.zeros((8, LANES), F32)] * NFIELD)
                )
                out_ref[pl.ds(t * 8 * SLAB + 8 + h, 8, stride=SLAB), :] = (code & 1023).astype(F32)
        for r in range(ntab):
            for t, h, weight, low, high, values in todo:
                here = high == r
                for f in range(NFIELD):
                    got = jnp.take_along_axis(tabs[f * ntab + r], low, axis=1)
                    values[f] = jnp.where(here, got, values[f])
        for t, h, weight, low, high, values in todo:
            for f in range(NFIELD):
                out_ref[pl.ds(t * 8 * SLAB + f * 2 + h, 8, stride=SLAB), :] = values[f] * weight

        def each(j, _):
            for t in turns:
                send(t * 8 + lax.rem(j + me, 8))
            return 0

        lax.fori_loop(0, 8, each, 0)
        return 0

    lax.fori_loop(0, trips, some, 0)


def scatter_phase(n, recv_ref, acc, group):
    one, zero = jnp.ones((), BF16), jnp.zeros((), BF16)
    acc[...] = jnp.zeros_like(acc)
    iota_a = (iota((16, LANES), 0) & 7).astype(F32).astype(BF16)
    iota_b = iota((LANES, LANES), 0).astype(F32).astype(BF16)

    def some(i, _):
        left = [[] for _ in range(4)]
        right = []
        for s in range(group):
            base = pl.multiple_of((i * group + s) * SLAB, 8)
            values = recv_ref[pl.ds(base, 8), :]
            cell = recv_ref[pl.ds(base + 8, 8), :].astype(I32)
            high = values.astype(BF16).astype(F32)
            low = values - high
            major = (cell >> 7).astype(F32)
            minor = (cell & 127).astype(F32)
            for h in range(2):
                hit = iota_a == jnp.broadcast_to(major[h : h + 1, :], (16, LANES)).astype(BF16)
                right.append(jnp.where(iota_b == thick(minor[h : h + 1, :], LANES), one, zero))
                for p, piece in enumerate((high, low)):
                    for g in range(2):
                        pair = jnp.concatenate(
                            [
                                jnp.broadcast_to(piece[f * 2 + h : f * 2 + h + 1, :], (8, LANES))
                                for f in (2 * g, 2 * g + 1)
                            ],
                            axis=0,
                        ).astype(BF16)
                        left[p * 2 + g].append(jnp.where(hit, pair, zero))
        lhs = jnp.concatenate([jnp.concatenate(part, axis=1) for part in left], axis=0)
        acc[...] += nt_dot(lhs, jnp.concatenate(right, axis=1))
        return 0

    lax.fori_loop(0, n // group, some, 0)


def stencil_phase(cells, coef_ref, nb_ref, total_ref, sten_h, sten_l):
    offset = [nb_ref[k : k + 1, :] for k in range(NEI)]
    weight = [coef_ref[k : k + 1, :] for k in range(NEI)]
    total = weight[0]
    for k in range(1, NEI):
        total = total + weight[k]
    total_ref[0:1, :] = total
    merged = []
    for k in range(NEI):
        w = weight[k]
        for j in range(k):
            w = w + jnp.where(offset[j] == offset[k], weight[j], 0.0)
        merged.append(w)
    local = lax.rem(iota((1, cells), 1), BLOCK) + HW
    target = [local + offset[k] for k in range(NEI)]
    for b in range(cells // BLOCK):
        cols = slice(b * BLOCK, (b + 1) * BLOCK)
        aim = [t[:, cols] for t in target]
        put = [w[:, cols] for w in merged]

        def one_band(i, _):
            at = pl.ds(pl.multiple_of(i * 128, 128), 128)
            row = iota((128, BLOCK), 0) + i * 128
            value = jnp.zeros((128, BLOCK), F32)
            for k in range(NEI):
                value = jnp.where(row == aim[k], put[k], value)
            high = value.astype(BF16)
            sten_h[b, at, :] = high
            sten_l[b, at, :] = (value - high.astype(F32)).astype(BF16)
            return 0

        lax.fori_loop(0, BAND // 128, one_band, 0)


def move_kernel(
    n, n_inner, levels, cells,
    dev_hbm, src_hbm, cell_hbm, w_hbm, atm_hbm,
    q_hbm, coef_hbm, nb_hbm, act_hbm, act8_hbm, bl8_hbm, kd_hbm, kv_hbm,
    z_out, e_out, r0_ref, flux_ref,
    z_ref, e_ref,
    dev_ref, src_ref, cell_ref, w_ref, atm_ref,
    q_ref, coef_ref, nb_ref, act_ref, act8_ref, bl8_ref, kd_ref, kv_ref,
    ranks, slots, tabs, packed, received, surface_acc,
    halo, q1, split, sten_h, sten_l, rates, recip, total_ref,
    halo_send, halo_recv, slab_send, slab_recv, own_sem, load_sem, out_sem, e_sem,
):
    tiles = cells // LANES
    me = lax.axis_index("grp") * n_inner + lax.axis_index("ocn")
    group_rows = NFIELD // 2 * levels

    def ident(d):
        return (d // n_inner, lax.rem(d, n_inner))

    barrier = pltpu.get_barrier_semaphore()

    my_outer = lax.axis_index("grp")
    my_inner = lax.axis_index("ocn")

    def greet(i, _):
        for g in range(n // n_inner):
            other = (lax.rem(my_outer + g, n // n_inner), lax.rem(my_inner + i, n_inner))

            def hello():
                pl.semaphore_signal(barrier, inc=1, device_id=other, device_id_type=MESH)

            if g == 0:
                pl.when(i != 0)(hello)
            else:
                hello()
        return 0

    loads = [
        pltpu.make_async_copy(source, target, load_sem.at[i])
        for i, (source, target) in enumerate(
            [
                (dev_hbm, dev_ref), (q_hbm, q_ref), (src_hbm, src_ref), (cell_hbm, cell_ref),
                (w_hbm, w_ref), (atm_hbm, atm_ref), (coef_hbm, coef_ref), (nb_hbm, nb_ref),
                (act_hbm, act_ref), (act8_hbm, act8_ref), (bl8_hbm, bl8_ref), (kd_hbm, kd_ref),
                (kv_hbm, kv_ref),
            ]
        )
    ]
    for load in loads:
        load.start()
    lax.fori_loop(0, n_inner, greet, 0, unroll=4)
    loads[0].wait()
    rank_phase(n, dev_ref, ranks, 32)

    def put_split(f, lanes, value):
        g = f // 2
        at = g * 2 * group_rows + (f % 2) * levels
        high = value.astype(BF16)
        split[pl.ds(at, levels), lanes] = high
        split[pl.ds(at + group_rows, levels), lanes] = (value - high.astype(F32)).astype(BF16)

    loads[1].wait()
    for f in range(NFIELD):
        put_split(f, pl.ds(HW, cells), q_ref[f])
    pl.semaphore_wait(barrier, n - 1)

    far = lax.rem(me, 2)
    near = 1 - far

    def halo_copy(step, side, g):
        source = q_ref if step == 0 else q1
        fields = pl.ds(2 * g, 2)
        return pltpu.make_async_remote_copy(
            src_ref=source.at[fields, :, pl.ds(pl.multiple_of(side * HW, HW), HW)],
            dst_ref=halo.at[step, 1 - side, fields],
            send_sem=halo_send.at[step, side, g],
            recv_sem=halo_recv.at[step, 1 - side, g],
            device_id=ident(lax.rem(me + n - 1 + 2 * side, n)),
            device_id_type=MESH,
        )

    for side in (far, near):
        for g in range(2):
            halo_copy(0, side, g).start()
    for load in loads[2:]:
        load.wait()
    place_phase(n, dev_ref, src_ref, cell_ref, w_ref, ranks, slots, 32)

    def slab_copy(d):
        return pltpu.make_async_remote_copy(
            src_ref=packed.at[pl.ds(pl.multiple_of(d * SLAB, 8), USED), :],
            dst_ref=received.at[pl.ds(pl.multiple_of(me * SLAB, 8), USED), :],
            send_sem=slab_send,
            recv_sem=slab_recv,
            device_id=ident(d),
            device_id_type=MESH,
        )

    def send_slab(d):
        @pl.when(d != me)
        def _():
            slab_copy(d).start()

    gather_phase(n, n_inner, me, atm_ref, slots, packed, tabs, send_slab)
    mine = pl.ds(pl.multiple_of(me * SLAB, 8), SLAB)
    own = pltpu.make_async_copy(packed.at[mine, :], received.at[mine, :], own_sem)
    own.start()

    stencil_phase(cells, coef_ref, nb_ref, total_ref, sten_h, sten_l)

    def advance(step, side, g):
        halo_copy(step, 1 - side, g).wait_recv()
        lanes = pl.ds(pl.multiple_of(side * (HW + cells), HW), HW)
        for f in (2 * g, 2 * g + 1):
            put_split(f, lanes, halo[step, side, f])
        source = q_ref if step == 0 else q1
        at = g * 2 * group_rows
        for k in range(HW // BLOCK):
            b = side * (HW // BLOCK) + k
            cols = pl.ds(pl.multiple_of(b * BLOCK, BLOCK), BLOCK)
            window = pl.ds(pl.multiple_of(b * BLOCK, BLOCK), BAND)
            both = jnp.dot(
                split[pl.ds(at, 2 * group_rows), window], sten_h[b], preferred_element_type=F32
            )
            extra = jnp.dot(
                split[pl.ds(at, group_rows), window], sten_l[b], preferred_element_type=F32
            )
            inflow = both[:group_rows] + both[group_rows:] + extra
            live = iota((levels, BLOCK), 0) < act_ref[:, cols]
            for f in (2 * g, 2 * g + 1):
                centre = source[f, :, cols]
                moved = (
                    centre
                    + inflow[(f % 2) * levels : (f % 2 + 1) * levels]
                    - centre * total_ref[0:1, cols]
                )
                moved = jnp.where(live, moved, centre)
                if step == 0:
                    q1[f, :, cols] = moved
                else:
                    for h in range(BLOCK // LANES):
                        z_ref[
                            pl.ds(f * levels * tiles + b * (BLOCK // LANES) + h, levels, stride=tiles), :
                        ] = moved[:, h * LANES : (h + 1) * LANES]
        if step == 0:
            halo_copy(1, side, g).start()

    for side in (near, far):
        for g in range(2):
            advance(0, side, g)
    for f in range(NFIELD):
        put_split(f, pl.ds(HW, cells), q1[f])

    for j in range(tiles):
        lanes = slice(j * LANES, (j + 1) * LANES)
        rates[pl.ds(j, levels, stride=tiles), :] = kd_ref[:, lanes]
        rates[pl.ds(levels * tiles + j, levels, stride=tiles), :] = kv_ref[:, lanes]
    active8 = act8_ref[...]
    bound8 = bl8_ref[...]

    def one_level(i, below):
        level = levels - 1 - i
        is_open = (active8 > level) & (level >= 1)
        inside = bound8 > level
        after = []
        for c in range(2):
            at = pl.ds(pl.multiple_of((c * levels + level) * tiles, 8), tiles)
            face = jnp.where(is_open, jnp.where(inside, rates[at, :], 0.05), 0.0)
            inverse = 1.0 / (1.0 + face + below[c])
            ratio = face * inverse
            recip[at, :] = inverse
            e_ref[at, :] = ratio
            after.append(face - face * ratio)
        return tuple(after)

    nothing = jnp.zeros((tiles, LANES), F32)
    lax.fori_loop(0, levels, one_level, (nothing, nothing), unroll=4)

    for g in range(2):
        advance(1, near, g)

    own.wait()
    everyone = pl.ds(0, (n - 1) * USED)
    arrived = pltpu.make_async_remote_copy(
        src_ref=packed.at[everyone, :],
        dst_ref=received.at[everyone, :],
        send_sem=slab_send,
        recv_sem=slab_recv,
        device_id=ident(lax.rem(me + 1, n)),
        device_id_type=MESH,
    )
    arrived.wait_recv()
    scatter_phase(n, received, surface_acc, 16)
    half = NFIELD * tiles
    surface = surface_acc[:half, :] + surface_acc[half:, :]
    flux_ref[...] = surface

    half_rows = 2 * levels * tiles

    def z_copy(g):
        at = pl.ds(g * half_rows, half_rows)
        return pltpu.make_async_copy(z_ref.at[at, :], z_out.at[at, :], out_sem.at[g])

    e_copy = pltpu.make_async_copy(e_ref, e_out, e_sem)
    e_copy.start()
    for c in range(2):
        r0_ref[c * tiles : (c + 1) * tiles, :] = recip[pl.ds(c * levels * tiles, tiles), :]

    for g in range(2):
        advance(1, far, g)
        fields = (2 * g, 2 * g + 1)

        def lift(i, above):
            level = levels - 1 - i
            own_at = pl.ds(pl.multiple_of((g * levels + level) * tiles, 8), tiles)
            after = []
            for f, carried in zip(fields, above):
                at = pl.ds(pl.multiple_of((f * levels + level) * tiles, 8), tiles)
                right_side = z_ref[at, :] + carried
                z_ref[at, :] = recip[own_at, :] * right_side
                after.append(e_ref[own_at, :] * right_side)
            return tuple(after)

        lax.fori_loop(0, levels, lift, (nothing,) * 2, unroll=8)
        z_copy(g).start()
    for g in range(2):
        z_copy(g).wait()
    e_copy.wait()
    arrived.wait_send()
    for step in range(ADV_STEPS):
        for side in range(2):
            for g in range(2):
                halo_copy(step, side, g).wait_send()


def finish_kernel(levels, cells, z_ref, e_ref, r0_ref, flux_ref, out_ref, surface_ref, state):
    tiles = cells // LANES
    g = pl.program_id(0)

    @pl.when(g == 0)
    def _():
        for f in range(NFIELD):
            for a in range(tiles):
                r = f * tiles + a
                surface_ref[f : f + 1, a * LANES : (a + 1) * LANES] = flux_ref[r : r + 1, :]

    below = []
    for f in range(2):
        at = pl.ds(f * levels * tiles, tiles)
        flux = flux_ref[pl.ds(pl.multiple_of((g * 2 + f) * tiles, 8), tiles), :]
        top = z_ref[at, :] + flux * r0_ref[...]
        state[at, :] = top
        below.append(top)

    def drop(level, above):
        own_at = pl.ds(pl.multiple_of(level * tiles, 8), tiles)
        after = []
        for f in range(2):
            at = pl.ds(pl.multiple_of((f * levels + level) * tiles, 8), tiles)
            value = z_ref[at, :] + e_ref[own_at, :] * above[f]
            state[at, :] = value
            after.append(value)
        return tuple(after)

    lax.fori_loop(1, levels, drop, tuple(below), unroll=8)
    for f in range(2):
        for j in range(tiles):
            out_ref[f, :, j * LANES : (j + 1) * LANES] = state[
                pl.ds(f * levels * tiles + j, levels, stride=tiles), :
            ]


def vmem(count):
    return [pl.BlockSpec(memory_space=pltpu.VMEM)] * count


def shaped(*shape):
    return jax.ShapeDtypeStruct(shape, F32)


def per_device(
    n, n_inner,
    ocean_state, adv_coef, neighbours, active_levels, boundary_level, kpp_diff, kpp_visc,
    atm_flux, pair_source, pair_weight, pair_device, pair_cell,
):
    levels, cells = ocean_state.shape[1:]
    tiles = cells // LANES
    pairs = pair_source.shape[0]
    wide = (pairs // LANES, LANES)
    rows_all = NFIELD * levels
    z, e, r0, flux = pl.pallas_call(
        functools.partial(move_kernel, n, n_inner, levels, cells),
        out_shape=(
            shaped(rows_all * tiles, LANES),
            shaped(2 * levels * tiles, LANES),
            shaped(2 * tiles, LANES),
            shaped(NFIELD * tiles, LANES),
        ),
        in_specs=[pl.BlockSpec(memory_space=pltpu.HBM)] * 13,
        out_specs=tuple([pl.BlockSpec(memory_space=pltpu.HBM)] * 2 + vmem(2)),
        scratch_shapes=[
            pltpu.VMEM((rows_all * tiles, LANES), F32),
            pltpu.VMEM((2 * levels * tiles, LANES), F32),
            pltpu.VMEM(wide, I32),
            pltpu.VMEM(wide, I32),
            pltpu.VMEM(wide, I32),
            pltpu.VMEM(wide, F32),
            pltpu.VMEM(atm_flux.shape, F32),
            pltpu.VMEM((NFIELD, levels, cells), F32),
            pltpu.VMEM((NEI, cells), F32),
            pltpu.VMEM((NEI, cells), I32),
            pltpu.VMEM((1, cells), I32),
            pltpu.VMEM((tiles, LANES), I32),
            pltpu.VMEM((tiles, LANES), I32),
            pltpu.VMEM((levels, cells), F32),
            pltpu.VMEM((levels, cells), F32),
            pltpu.VMEM(wide, F32),
            pltpu.VMEM((5 * n, SLOTS), F32),
            pltpu.VMEM((NFIELD * atm_flux.shape[1] // LANES, 8, LANES), F32),
            pltpu.VMEM((n * SLAB, LANES), F32),
            pltpu.VMEM((n * SLAB, LANES), F32),
            pltpu.VMEM((2 * NFIELD * tiles, LANES), F32),
            pltpu.VMEM((ADV_STEPS, 2, NFIELD, levels, HW), F32),
            pltpu.VMEM((NFIELD, levels, cells), F32),
            pltpu.VMEM((2 * rows_all, cells + 2 * HW), BF16),
            pltpu.VMEM((cells // BLOCK, BAND, BLOCK), BF16),
            pltpu.VMEM((cells // BLOCK, BAND, BLOCK), BF16),
            pltpu.VMEM((2 * levels * tiles, LANES), F32),
            pltpu.VMEM((2 * levels * tiles, LANES), F32),
            pltpu.VMEM((8, cells), F32),
            pltpu.SemaphoreType.DMA((ADV_STEPS, 2, 2)),
            pltpu.SemaphoreType.DMA((ADV_STEPS, 2, 2)),
            pltpu.SemaphoreType.DMA,
            pltpu.SemaphoreType.DMA,
            pltpu.SemaphoreType.DMA,
            pltpu.SemaphoreType.DMA((13,)),
            pltpu.SemaphoreType.DMA((2,)),
            pltpu.SemaphoreType.DMA,
        ],
        compiler_params=pltpu.CompilerParams(
            vmem_limit_bytes=63 * 1024 * 1024, collective_id=0, has_side_effects=True
        ),
        name="move",
    )(
        pair_device.reshape(wide), pair_source.reshape(wide), pair_cell.reshape(wide),
        pair_weight.reshape(wide), atm_flux,
        ocean_state, adv_coef, neighbours, active_levels.reshape(1, cells),
        active_levels.reshape(tiles, LANES), boundary_level.reshape(tiles, LANES),
        kpp_diff, kpp_visc,
    )
    half = 2 * levels * tiles
    return pl.pallas_call(
        functools.partial(finish_kernel, levels, cells),
        grid=(2,),
        out_shape=(shaped(NFIELD, levels, cells), shaped(NFIELD, cells)),
        in_specs=[
            pl.BlockSpec((half, LANES), lambda g: (g, 0)),
            pl.BlockSpec((levels * tiles, LANES), lambda g: (g, 0)),
            pl.BlockSpec((tiles, LANES), lambda g: (g, 0)),
            pl.BlockSpec((NFIELD * tiles, LANES), lambda g: (0, 0)),
        ],
        out_specs=(
            pl.BlockSpec((2, levels, cells), lambda g: (g, 0, 0)),
            pl.BlockSpec((NFIELD, cells), lambda g: (0, 0)),
        ),
        scratch_shapes=[pltpu.VMEM((half, LANES), F32)],
        compiler_params=pltpu.CompilerParams(vmem_limit_bytes=63 * 1024 * 1024),
        name="finish",
    )(z, e, r0, flux)


def solution(mesh):
    both = ("grp", "ocn")
    placed = (
        P(None, None, both), P(None, both), P(None, both), P(both), P(both), P(None, both),
        P(None, both), P(None, both), P(both), P(both), P(both, None), P(both),
    )
    n_inner = mesh.shape["ocn"]
    return jax.shard_map(
        functools.partial(per_device, mesh.shape["grp"] * n_inner, n_inner),
        mesh=mesh,
        in_specs=placed,
        out_specs=(P(None, None, both), P(None, both)),
        check_vma=False,
    )
```

```python
import functools

import jax
import jax.numpy as jnp
from jax import lax
from jax.experimental import pallas as pl
from jax.experimental.pallas import tpu as pltpu
from jax.sharding import PartitionSpec as P

NFIELD = 4
NEI = 6
HW = 512
ADV_STEPS = 2
SLOTS = 256
LANES = 128
SLAB = 16
USED = 10
BLOCK = 256
BAND = BLOCK + 2 * HW
MESH = pl.DeviceIdType.MESH
F32 = jnp.float32
BF16 = jnp.bfloat16
I32 = jnp.int32


def iota(shape, dim):
    return lax.broadcasted_iota(I32, shape, dim)


def nt_dot(a, b):
    return lax.dot_general(a, b, (((1,), (1,)), ((), ())), preferred_element_type=F32)


def thick(row, count):
    sixteen = jnp.broadcast_to(row, (16, LANES)).astype(BF16)
    return jnp.broadcast_to(sixteen[None], (count // 16, 16, LANES)).reshape(count, LANES)


def rank_phase(n, dev_ref, ranks, chunk):
    iota_d = iota((n, LANES), 0)
    tri = jnp.where(iota((256, 256), 0) <= iota((256, 256), 1), 1.0, 0.0).astype(BF16)

    def some(i, run):
        at = pl.ds(pl.multiple_of(i * chunk, 8), chunk)
        dest = dev_ref[at, :]
        out = []
        for s in range(0, chunk, 2):
            hit = [iota_d == dest[s + h : s + h + 1, :] for h in range(2)]
            member = jnp.concatenate([jnp.where(m, 1.0, 0.0) for m in hit], axis=1).astype(BF16)
            count = jnp.dot(member, tri, preferred_element_type=F32)
            for h in range(2):
                upto = count[:, h * LANES : (h + 1) * LANES] + run
                out.append(jnp.sum(jnp.where(hit[h], upto, 0.0), axis=0, keepdims=True) - 1.0)
            run = run + jnp.broadcast_to(count[:, 255:256], (n, LANES))
        ranks[at, :] = jnp.concatenate(out, axis=0)
        return run

    lax.fori_loop(0, dev_ref.shape[0] // chunk, some, jnp.zeros((n, LANES), F32))


def place_phase(n, dev_ref, src_ref, cell_ref, w_ref, ranks, acc, chunk):
    one, zero = jnp.ones((), BF16), jnp.zeros((), BF16)
    iota_d = iota((n, LANES), 0).astype(F32).astype(BF16)
    iota_r = iota((SLOTS, LANES), 0).astype(F32).astype(BF16)
    acc[...] = jnp.zeros_like(acc)

    def some(i, _):
        at = pl.ds(pl.multiple_of(i * chunk, 8), chunk)
        dest = dev_ref[at, :].astype(F32)
        code = src_ref[at, :] * 1024 + cell_ref[at, :]
        weight = w_ref[at, :]
        rank = ranks[at, :]
        high = weight.astype(BF16).astype(F32)
        pieces = [
            (code & 127).astype(F32),
            ((code >> 7) & 127).astype(F32),
            (code >> 14).astype(F32),
            high,
            weight - high,
        ]
        left = [[] for _ in pieces]
        right = []
        for s in range(chunk):
            mask = iota_d == thick(dest[s : s + 1, :], n)
            right.append(jnp.where(iota_r == thick(rank[s : s + 1, :], SLOTS), one, zero))
            for v, piece in enumerate(pieces):
                left[v].append(jnp.where(mask, thick(piece[s : s + 1, :], n), zero))
        lhs = jnp.concatenate([jnp.concatenate(part, axis=1) for part in left], axis=0)
        acc[...] += nt_dot(lhs, jnp.concatenate(right, axis=1))
        return 0

    lax.fori_loop(0, dev_ref.shape[0] // chunk, some, 0)


def gather_phase(n, n_inner, me, atm_ref, acc, out_ref, tabs, send):
    ntab = atm_ref.shape[1] // LANES
    tiles = 2
    trips = n // (8 * tiles)
    outer = n // n_inner
    inner = n_inner // 8
    for f in range(NFIELD):
        for r in range(ntab):
            tabs[f * ntab + r] = jnp.broadcast_to(
                atm_ref[f : f + 1, r * LANES : (r + 1) * LANES], (8, LANES)
            )

    def some(i, _):
        todo = []
        turns = []
        for u in range(tiles):
            m = i * tiles + u
            up = lax.rem(m, outer)
            across = m // outer + inner // 2 * lax.rem(up, 2) + up // 2
            t = lax.rem(me // n_inner + up, outer) * inner + lax.rem(
                lax.rem(me, n_inner) // 8 + across, inner
            )
            turns.append(t)
            for h in range(2):
                lanes = slice(h * LANES, (h + 1) * LANES)

                def part(v):
                    return acc[pl.ds(pl.multiple_of(v * n + t * 8, 8), 8), lanes]

                code = (part(0) + part(1) * 128.0 + part(2) * 16384.0).astype(I32)
                weight = part(3) + part(4)
                source = code >> 10
                todo.append(
                    (t, h, weight, source & (LANES - 1), source >> 7,
                     [jnp.zeros((8, LANES), F32)] * NFIELD)
                )
                out_ref[pl.ds(t * 8 * SLAB + 8 + h, 8, stride=SLAB), :] = (code & 1023).astype(F32)
        for r in range(ntab):
            for t, h, weight, low, high, values in todo:
                here = high == r
                for f in range(NFIELD):
                    got = jnp.take_along_axis(tabs[f * ntab + r], low, axis=1)
                    values[f] = jnp.where(here, got, values[f])
        for t, h, weight, low, high, values in todo:
            for f in range(NFIELD):
                out_ref[pl.ds(t * 8 * SLAB + f * 2 + h, 8, stride=SLAB), :] = values[f] * weight

        def each(j, _):
            for t in turns:
                send(t * 8 + lax.rem(j + me, 8))
            return 0

        lax.fori_loop(0, 8, each, 0)
        return 0

    lax.fori_loop(0, trips, some, 0)


def scatter_phase(n, recv_ref, acc, group):
    one, zero = jnp.ones((), BF16), jnp.zeros((), BF16)
    acc[...] = jnp.zeros_like(acc)
    iota_a = (iota((16, LANES), 0) & 7).astype(F32).astype(BF16)
    iota_b = iota((LANES, LANES), 0).astype(F32).astype(BF16)

    def some(i, _):
        left = [[] for _ in range(4)]
        right = []
        for s in range(group):
            base = pl.multiple_of((i * group + s) * SLAB, 8)
            values = recv_ref[pl.ds(base, 8), :]
            cell = recv_ref[pl.ds(base + 8, 8), :].astype(I32)
            high = values.astype(BF16).astype(F32)
            low = values - high
            major = (cell >> 7).astype(F32)
            minor = (cell & 127).astype(F32)
            for h in range(2):
                hit = iota_a == jnp.broadcast_to(major[h : h + 1, :], (16, LANES)).astype(BF16)
                right.append(jnp.where(iota_b == thick(minor[h : h + 1, :], LANES), one, zero))
                for p, piece in enumerate((high, low)):
                    for g in range(2):
                        pair = jnp.concatenate(
                            [
                                jnp.broadcast_to(piece[f * 2 + h : f * 2 + h + 1, :], (8, LANES))
                                for f in (2 * g, 2 * g + 1)
                            ],
                            axis=0,
                        ).astype(BF16)
                        left[p * 2 + g].append(jnp.where(hit, pair, zero))
        lhs = jnp.concatenate([jnp.concatenate(part, axis=1) for part in left], axis=0)
        acc[...] += nt_dot(lhs, jnp.concatenate(right, axis=1))
        return 0

    lax.fori_loop(0, n // group, some, 0)


def stencil_phase(cells, coef_ref, nb_ref, total_ref, sten_h, sten_l):
    offset = [nb_ref[k : k + 1, :] for k in range(NEI)]
    weight = [coef_ref[k : k + 1, :] for k in range(NEI)]
    total = weight[0]
    for k in range(1, NEI):
        total = total + weight[k]
    total_ref[0:1, :] = total
    merged = []
    for k in range(NEI):
        w = weight[k]
        for j in range(k):
            w = w + jnp.where(offset[j] == offset[k], weight[j], 0.0)
        merged.append(w)
    local = lax.rem(iota((1, cells), 1), BLOCK) + HW
    target = [local + offset[k] for k in range(NEI)]
    for b in range(cells // BLOCK):
        cols = slice(b * BLOCK, (b + 1) * BLOCK)
        aim = [t[:, cols] for t in target]
        put = [w[:, cols] for w in merged]

        def one_band(i, _):
            at = pl.ds(pl.multiple_of(i * 128, 128), 128)
            row = iota((128, BLOCK), 0) + i * 128
            value = jnp.zeros((128, BLOCK), F32)
            for k in range(NEI):
                value = jnp.where(row == aim[k], put[k], value)
            high = value.astype(BF16)
            sten_h[b, at, :] = high
            sten_l[b, at, :] = (value - high.astype(F32)).astype(BF16)
            return 0

        lax.fori_loop(0, BAND // 128, one_band, 0)


def move_kernel(
    n, n_inner, levels, cells,
    dev_hbm, src_hbm, cell_hbm, w_hbm, atm_hbm,
    q_hbm, coef_hbm, nb_hbm, act_hbm, act8_hbm, bl8_hbm, kd_hbm, kv_hbm,
    z_out, e_out, r0_ref, flux_ref,
    z_ref, e_ref,
    dev_ref, src_ref, cell_ref, w_ref, atm_ref,
    q_ref, coef_ref, nb_ref, act_ref, act8_ref, bl8_ref, kd_ref, kv_ref,
    ranks, slots, tabs, packed, received, surface_acc,
    halo, q1, split, sten_h, sten_l, rates, recip, total_ref,
    halo_send, halo_recv, slab_send, slab_recv, own_sem, load_sem, out_sem, e_sem,
):
    tiles = cells // LANES
    me = lax.axis_index("grp") * n_inner + lax.axis_index("ocn")
    group_rows = NFIELD // 2 * levels

    def ident(d):
        return (d // n_inner, lax.rem(d, n_inner))

    barrier = pltpu.get_barrier_semaphore()

    my_outer = lax.axis_index("grp")
    my_inner = lax.axis_index("ocn")

    def greet(i, _):
        for g in range(n // n_inner):
            other = (lax.rem(my_outer + g, n // n_inner), lax.rem(my_inner + i, n_inner))

            def hello():
                pl.semaphore_signal(barrier, inc=1, device_id=other, device_id_type=MESH)

            if g == 0:
                pl.when(i != 0)(hello)
            else:
                hello()
        return 0

    loads = [
        pltpu.make_async_copy(source, target, load_sem.at[i])
        for i, (source, target) in enumerate(
            [
                (dev_hbm, dev_ref), (q_hbm, q_ref), (src_hbm, src_ref), (cell_hbm, cell_ref),
                (w_hbm, w_ref), (atm_hbm, atm_ref), (coef_hbm, coef_ref), (nb_hbm, nb_ref),
                (act_hbm, act_ref), (act8_hbm, act8_ref), (bl8_hbm, bl8_ref), (kd_hbm, kd_ref),
                (kv_hbm, kv_ref),
            ]
        )
    ]
    for load in loads:
        load.start()
    lax.fori_loop(0, n_inner, greet, 0, unroll=4)
    loads[0].wait()
    rank_phase(n, dev_ref, ranks, 32)

    def put_split(f, lanes, value):
        g = f // 2
        at = g * 2 * group_rows + (f % 2) * levels
        high = value.astype(BF16)
        split[pl.ds(at, levels), lanes] = high
        split[pl.ds(at + group_rows, levels), lanes] = (value - high.astype(F32)).astype(BF16)

    loads[1].wait()
    for f in range(NFIELD):
        put_split(f, pl.ds(HW, cells), q_ref[f])
    pl.semaphore_wait(barrier, n - 1)

    far = lax.rem(me, 2)
    near = 1 - far

    def halo_copy(step, side, g):
        source = q_ref if step == 0 else q1
        fields = pl.ds(2 * g, 2)
        return pltpu.make_async_remote_copy(
            src_ref=source.at[fields, :, pl.ds(pl.multiple_of(side * HW, HW), HW)],
            dst_ref=halo.at[step, 1 - side, fields],
            send_sem=halo_send.at[step, side, g],
            recv_sem=halo_recv.at[step, 1 - side, g],
            device_id=ident(lax.rem(me + n - 1 + 2 * side, n)),
            device_id_type=MESH,
        )

    for side in (far, near):
        for g in range(2):
            halo_copy(0, side, g).start()
    for load in loads[2:]:
        load.wait()
    place_phase(n, dev_ref, src_ref, cell_ref, w_ref, ranks, slots, 32)

    def slab_copy(d):
        return pltpu.make_async_remote_copy(
            src_ref=packed.at[pl.ds(pl.multiple_of(d * SLAB, 8), USED), :],
            dst_ref=received.at[pl.ds(pl.multiple_of(me * SLAB, 8), USED), :],
            send_sem=slab_send,
            recv_sem=slab_recv,
            device_id=ident(d),
            device_id_type=MESH,
        )

    def send_slab(d):
        @pl.when(d != me)
        def _():
            slab_copy(d).start()

    gather_phase(n, n_inner, me, atm_ref, slots, packed, tabs, send_slab)
    mine = pl.ds(pl.multiple_of(me * SLAB, 8), SLAB)
    own = pltpu.make_async_copy(packed.at[mine, :], received.at[mine, :], own_sem)
    own.start()

    stencil_phase(cells, coef_ref, nb_ref, total_ref, sten_h, sten_l)

    def advance(step, side, g):
        halo_copy(step, 1 - side, g).wait_recv()
        lanes = pl.ds(pl.multiple_of(side * (HW + cells), HW), HW)
        for f in (2 * g, 2 * g + 1):
            put_split(f, lanes, halo[step, side, f])
        source = q_ref if step == 0 else q1
        at = g * 2 * group_rows
        for k in range(HW // BLOCK):
            b = side * (HW // BLOCK) + k
            cols = pl.ds(pl.multiple_of(b * BLOCK, BLOCK), BLOCK)
            window = pl.ds(pl.multiple_of(b * BLOCK, BLOCK), BAND)
            both = jnp.dot(
                split[pl.ds(at, 2 * group_rows), window], sten_h[b], preferred_element_type=F32
            )
            extra = jnp.dot(
                split[pl.ds(at, group_rows), window], sten_l[b], preferred_element_type=F32
            )
            inflow = both[:group_rows] + both[group_rows:] + extra
            live = iota((levels, BLOCK), 0) < act_ref[:, cols]
            for f in (2 * g, 2 * g + 1):
                centre = source[f, :, cols]
                moved = (
                    centre
                    + inflow[(f % 2) * levels : (f % 2 + 1) * levels]
                    - centre * total_ref[0:1, cols]
                )
                moved = jnp.where(live, moved, centre)
                if step == 0:
                    q1[f, :, cols] = moved
                else:
                    for h in range(BLOCK // LANES):
                        z_ref[
                            pl.ds(f * levels * tiles + b * (BLOCK // LANES) + h, levels, stride=tiles), :
                        ] = moved[:, h * LANES : (h + 1) * LANES]
        if step == 0:
            halo_copy(1, side, g).start()

    for side in (near, far):
        for g in range(2):
            advance(0, side, g)
    for f in range(NFIELD):
        put_split(f, pl.ds(HW, cells), q1[f])

    for j in range(tiles):
        lanes = slice(j * LANES, (j + 1) * LANES)
        rates[pl.ds(j, levels, stride=tiles), :] = kd_ref[:, lanes]
        rates[pl.ds(levels * tiles + j, levels, stride=tiles), :] = kv_ref[:, lanes]
    active8 = act8_ref[...]
    bound8 = bl8_ref[...]

    def one_level(i, below):
        level = levels - 1 - i
        is_open = (active8 > level) & (level >= 1)
        inside = bound8 > level
        after = []
        for c in range(2):
            at = pl.ds(pl.multiple_of((c * levels + level) * tiles, 8), tiles)
            face = jnp.where(is_open, jnp.where(inside, rates[at, :], 0.05), 0.0)
            inverse = 1.0 / (1.0 + face + below[c])
            ratio = face * inverse
            recip[at, :] = inverse
            e_ref[at, :] = ratio
            after.append(face - face * ratio)
        return tuple(after)

    nothing = jnp.zeros((tiles, LANES), F32)
    lax.fori_loop(0, levels, one_level, (nothing, nothing), unroll=4)

    for g in range(2):
        advance(1, near, g)

    own.wait()
    everyone = pl.ds(0, (n - 1) * USED)
    arrived = pltpu.make_async_remote_copy(
        src_ref=packed.at[everyone, :],
        dst_ref=received.at[everyone, :],
        send_sem=slab_send,
        recv_sem=slab_recv,
        device_id=ident(lax.rem(me + 1, n)),
        device_id_type=MESH,
    )
    arrived.wait_recv()
    scatter_phase(n, received, surface_acc, 16)
    half = NFIELD * tiles
    surface = surface_acc[:half, :] + surface_acc[half:, :]
    flux_ref[...] = surface

    half_rows = 2 * levels * tiles

    def z_copy(g):
        at = pl.ds(g * half_rows, half_rows)
        return pltpu.make_async_copy(z_ref.at[at, :], z_out.at[at, :], out_sem.at[g])

    e_copy = pltpu.make_async_copy(e_ref, e_out, e_sem)
    e_copy.start()
    for c in range(2):
        r0_ref[c * tiles : (c + 1) * tiles, :] = recip[pl.ds(c * levels * tiles, tiles), :]

    for g in range(2):
        advance(1, far, g)
        fields = (2 * g, 2 * g + 1)

        def lift(i, above):
            level = levels - 1 - i
            own_at = pl.ds(pl.multiple_of((g * levels + level) * tiles, 8), tiles)
            after = []
            for f, carried in zip(fields, above):
                at = pl.ds(pl.multiple_of((f * levels + level) * tiles, 8), tiles)
                right_side = z_ref[at, :] + carried
                z_ref[at, :] = recip[own_at, :] * right_side
                after.append(e_ref[own_at, :] * right_side)
            return tuple(after)

        lax.fori_loop(0, levels, lift, (nothing,) * 2, unroll=8)
        z_copy(g).start()
    for g in range(2):
        z_copy(g).wait()
    e_copy.wait()
    arrived.wait_send()
    for step in range(ADV_STEPS):
        for side in range(2):
            for g in range(2):
                halo_copy(step, side, g).wait_send()


def finish_kernel(levels, cells, z_ref, e_ref, r0_ref, flux_ref, out_ref, surface_ref, state):
    tiles = cells // LANES
    g = pl.program_id(0)

    @pl.when(g == 0)
    def _():
        for f in range(NFIELD):
            for a in range(tiles):
                r = f * tiles + a
                surface_ref[f : f + 1, a * LANES : (a + 1) * LANES] = flux_ref[r : r + 1, :]

    below = []
    for f in range(2):
        at = pl.ds(f * levels * tiles, tiles)
        flux = flux_ref[pl.ds(pl.multiple_of((g * 2 + f) * tiles, 8), tiles), :]
        top = z_ref[at, :] + flux * r0_ref[...]
        state[at, :] = top
        below.append(top)

    def drop(level, above):
        own_at = pl.ds(pl.multiple_of(level * tiles, 8), tiles)
        after = []
        for f in range(2):
            at = pl.ds(pl.multiple_of((f * levels + level) * tiles, 8), tiles)
            value = z_ref[at, :] + e_ref[own_at, :] * above[f]
            state[at, :] = value
            after.append(value)
        return tuple(after)

    lax.fori_loop(1, levels, drop, tuple(below), unroll=8)
    for f in range(2):
        for j in range(tiles):
            out_ref[f, :, j * LANES : (j + 1) * LANES] = state[
                pl.ds(f * levels * tiles + j, levels, stride=tiles), :
            ]


def vmem(count):
    return [pl.BlockSpec(memory_space=pltpu.VMEM)] * count


def shaped(*shape):
    return jax.ShapeDtypeStruct(shape, F32)


def per_device(
    n, n_inner,
    ocean_state, adv_coef, neighbours, active_levels, boundary_level, kpp_diff, kpp_visc,
    atm_flux, pair_source, pair_weight, pair_device, pair_cell,
):
    levels, cells = ocean_state.shape[1:]
    tiles = cells // LANES
    pairs = pair_source.shape[0]
    wide = (pairs // LANES, LANES)
    rows_all = NFIELD * levels
    z, e, r0, flux = pl.pallas_call(
        functools.partial(move_kernel, n, n_inner, levels, cells),
        out_shape=(
            shaped(rows_all * tiles, LANES),
            shaped(2 * levels * tiles, LANES),
            shaped(2 * tiles, LANES),
            shaped(NFIELD * tiles, LANES),
        ),
        in_specs=[pl.BlockSpec(memory_space=pltpu.HBM)] * 13,
        out_specs=tuple([pl.BlockSpec(memory_space=pltpu.HBM)] * 2 + vmem(2)),
        scratch_shapes=[
            pltpu.VMEM((rows_all * tiles + 8, LANES), F32),
            pltpu.VMEM((2 * levels * tiles, LANES), F32),
            pltpu.VMEM(wide, I32),
            pltpu.VMEM(wide, I32),
            pltpu.VMEM(wide, I32),
            pltpu.VMEM(wide, F32),
            pltpu.VMEM(atm_flux.shape, F32),
            pltpu.VMEM((NFIELD, levels, cells), F32),
            pltpu.VMEM((NEI, cells), F32),
            pltpu.VMEM((NEI, cells), I32),
            pltpu.VMEM((1, cells), I32),
            pltpu.VMEM((tiles, LANES), I32),
            pltpu.VMEM((tiles, LANES), I32),
            pltpu.VMEM((levels, cells), F32),
            pltpu.VMEM((levels, cells), F32),
            pltpu.VMEM(wide, F32),
            pltpu.VMEM((5 * n, SLOTS), F32),
            pltpu.VMEM((NFIELD * atm_flux.shape[1] // LANES, 8, LANES), F32),
            pltpu.VMEM((n * SLAB + SLAB, LANES), F32),
            pltpu.VMEM((n * SLAB, LANES), F32),
            pltpu.VMEM((2 * NFIELD * tiles, LANES), F32),
            pltpu.VMEM((ADV_STEPS, 2, NFIELD, levels, HW), F32),
            pltpu.VMEM((NFIELD, levels, cells), F32),
            pltpu.VMEM((2 * rows_all, cells + 2 * HW), BF16),
            pltpu.VMEM((cells // BLOCK, BAND, BLOCK), BF16),
            pltpu.VMEM((cells // BLOCK, BAND, BLOCK), BF16),
            pltpu.VMEM((2 * levels * tiles + 8, LANES), F32),
            pltpu.VMEM((2 * levels * tiles, LANES), F32),
            pltpu.VMEM((8, cells), F32),
            pltpu.SemaphoreType.DMA((ADV_STEPS, 2, 2)),
            pltpu.SemaphoreType.DMA((ADV_STEPS, 2, 2)),
            pltpu.SemaphoreType.DMA,
            pltpu.SemaphoreType.DMA,
            pltpu.SemaphoreType.DMA,
            pltpu.SemaphoreType.DMA((13,)),
            pltpu.SemaphoreType.DMA((2,)),
            pltpu.SemaphoreType.DMA,
        ],
        compiler_params=pltpu.CompilerParams(
            vmem_limit_bytes=63 * 1024 * 1024, collective_id=0, has_side_effects=True
        ),
        name="move",
    )(
        pair_device.reshape(wide), pair_source.reshape(wide), pair_cell.reshape(wide),
        pair_weight.reshape(wide), atm_flux,
        ocean_state, adv_coef, neighbours, active_levels.reshape(1, cells),
        active_levels.reshape(tiles, LANES), boundary_level.reshape(tiles, LANES),
        kpp_diff, kpp_visc,
    )
    half = 2 * levels * tiles
    return pl.pallas_call(
        functools.partial(finish_kernel, levels, cells),
        grid=(2,),
        out_shape=(shaped(NFIELD, levels, cells), shaped(NFIELD, cells)),
        in_specs=[
            pl.BlockSpec((half, LANES), lambda g: (g, 0)),
            pl.BlockSpec((levels * tiles, LANES), lambda g: (g, 0)),
            pl.BlockSpec((tiles, LANES), lambda g: (g, 0)),
            pl.BlockSpec((NFIELD * tiles, LANES), lambda g: (0, 0)),
        ],
        out_specs=(
            pl.BlockSpec((2, levels, cells), lambda g: (g, 0, 0)),
            pl.BlockSpec((NFIELD, cells), lambda g: (0, 0)),
        ),
        scratch_shapes=[pltpu.VMEM((half + 8, LANES), F32)],
        compiler_params=pltpu.CompilerParams(vmem_limit_bytes=63 * 1024 * 1024),
        name="finish",
    )(z, e, r0, flux)


def solution(mesh):
    both = ("grp", "ocn")
    placed = (
        P(None, None, both), P(None, both), P(None, both), P(both), P(both), P(None, both),
        P(None, both), P(None, both), P(both), P(both), P(both, None), P(both),
    )
    n_inner = mesh.shape["ocn"]
    return jax.shard_map(
        functools.partial(per_device, mesh.shape["grp"] * n_inner, n_inner),
        mesh=mesh,
        in_specs=placed,
        out_specs=(P(None, None, both), P(None, both)),
        check_vma=False,
    )
```
